1024 devices in a mesh: gx: 64 (over z, x_hi), gy: 16 (over y, x_lo, core).
Axes of the slice: x: 4 (x_hi: 2, x_lo: 2; x = x_hi * 2 + x_lo), y: 4, z: 32, core: 2. Of those that a mesh axis runs over, the one named last changes fastest.
Arguments:
- right_side: float32 [512, 256, 256], P('gx', 'gy'), may hold values from -8 to 8
- shift: float32 [512, 256, 256], P('gx', 'gy'), may hold values from 0.05 to 0.5
- coef_x: float32 [512, 256, 256], P('gx', 'gy'), may hold values from 0.5 to 2
- coef_y: float32 [512, 256, 256], P('gx', 'gy'), may hold values from 0.5 to 2
- coef_z: float32 [512, 256, 256], P('gx', 'gy'), may hold values from 0.5 to 2
- low_frac: float32 [2], replicated, may hold values from 0.01 to 0.05
- high_frac: float32 [2], replicated, may hold values from 1 to 1.3
Outputs:
- pressure: float32 [512, 256, 256], P('gx', 'gy')
- residual: float32 [512, 256, 256], P('gx', 'gy')
The draws below stay inside these ranges and needn't reach their ends.
All inputs are finite; a program needn't handle non-finite values.
Results may differ from the reference program's by a relative error of at most 0.000065.
Values sent between devices are 32-bit elements; how exact they have to be, the bound alone decides.
No kernel may reach another device: no remote copies, remote signals or barrier semaphores. Data moves between devices by JAX's collectives and lax.ppermute only.
A program may use at most 32 MiB of HBM per device.

```python
import math
import jax
import jax.numpy as jnp

NZ = 256
ITERS = 8
NX = 512
NY = 256


def steps_of(rng, dims, shards, smallest, top_value):
    def one(axis_at, parts):
        steps = jax.random.uniform(jax.random.fold_in(jax.random.fold_in(rng, 6), axis_at), (parts,), jnp.float32, smallest / len(shards), top_value / len(shards))
        return jnp.repeat(jnp.exp(steps), dims[axis_at] // parts).reshape((-1,) + (1,) * (len(dims) - axis_at - 1))

    level = one(*shards[0])
    for cut in shards[1:]:
        level = level * one(*cut)
    return level


def normal_values(key, extent, scale, most, shards=(), kind=jnp.bfloat16):
    level = steps_of(key, extent, shards, -0.22, 0.18) if shards else 1.0
    result = jax.random.normal(key, extent, jnp.float32) * scale * level
    return jnp.minimum(jnp.maximum(result, -most), most).astype(kind)


def setup_inputs(seed: int = 0) -> dict:
    key_of = jax.random.split(jax.random.key(seed), 8)
    return {
        "right_side": normal_values(key_of[0], (NX, NY, NZ), 1.0, 8.0, ((0, 64), (1, 16)), jnp.float32),
        "shift": jnp.clip(jnp.exp(math.log(0.5) - 2.3025851 * jax.random.uniform(key_of[1], (NX, NY, NZ), jnp.float32) ** steps_of(key_of[1], (NX, NY, NZ), ((0, 64), (1, 16)), -0.2, 0.2)), 0.05, 0.5),
        "coef_x": jnp.clip(jnp.exp(math.log(2.0) - 1.3862944 * jax.random.uniform(key_of[2], (NX, NY, NZ), jnp.float32) ** steps_of(key_of[2], (NX, NY, NZ), ((0, 64), (1, 16)), -0.2, 0.2)), 0.5, 2.0),
        "coef_y": jnp.clip(jnp.exp(math.log(2.0) - 1.3862944 * jax.random.uniform(key_of[3], (NX, NY, NZ), jnp.float32) ** steps_of(key_of[3], (NX, NY, NZ), ((0, 64), (1, 16)), -0.2, 0.2)), 0.5, 2.0),
        "coef_z": jnp.clip(jnp.exp(math.log(2.0) - 1.3862944 * jax.random.uniform(key_of[4], (NX, NY, NZ), jnp.float32) ** steps_of(key_of[4], (NX, NY, NZ), ((0, 64), (1, 16)), -0.2, 0.2)), 0.5, 2.0),
        "low_frac": jnp.clip(jax.random.uniform(key_of[5], (2,), jnp.float32, 0.01, 0.05), 0.01, 0.05),
        "high_frac": jnp.clip(jax.random.uniform(key_of[6], (2,), jnp.float32, 1.0, 1.3), 1.0, 1.3),
    }


def lower(a, axis):
    width = [(0, 0)] * a.ndim
    width[axis] = (1, 0)
    return jnp.pad(a, width)[tuple(slice(0, -1) if k == axis else slice(None) for k in range(a.ndim))]


def upper(a, axis):
    width = [(0, 0)] * a.ndim
    width[axis] = (0, 1)
    return jnp.pad(a, width)[tuple(slice(1, None) if k == axis else slice(None) for k in range(a.ndim))]


def operate(field, shift, coef_x, coef_y, coef_z, low_x, low_y, low_z):
    total = shift * field
    total = total + coef_x * (field - upper(field, 1)) + low_x * (field - lower(field, 1))
    total = total + coef_y * (field - upper(field, 2)) + low_y * (field - lower(field, 2))
    total = total + coef_z * (field - upper(field, 3)) + low_z * (field - lower(field, 3))
    return total


def reference(right_side, shift, coef_x, coef_y, coef_z, low_frac, high_frac):
    low_x = lower(coef_x, 0)
    low_y = lower(coef_y, 1)
    low_z = lower(coef_z, 2)
    bound = jnp.max(shift + 2.0 * (coef_x + low_x + coef_y + low_y + coef_z + low_z))
    mirrored = jnp.flip(right_side, 0)
    fields = jnp.stack([(right_side + mirrored) / 2.0, (right_side - mirrored) / 2.0])
    lmin = (low_frac * bound)[:, None, None, None]
    lmax = (high_frac * bound)[:, None, None, None]
    theta = (lmax + lmin) / 2.0
    delta = (lmax - lmin) / 2.0
    sigma = theta / delta
    rho = 1.0 / sigma
    solution = jnp.zeros_like(fields)
    resid = fields
    direction = resid / theta
    for step in range(ITERS):
        solution = solution + direction
        resid = resid - operate(direction, shift, coef_x, coef_y, coef_z, low_x, low_y, low_z)
        rho_new = 1.0 / (2.0 * sigma - rho)
        direction = rho_new * rho * direction + (2.0 * rho_new / delta) * resid
        rho = rho_new
    return solution[0] + solution[1], resid[0] + resid[1]
```

```python
import jax
import jax.numpy as jnp
from jax import lax
from jax.experimental import pallas as pl
from jax.experimental.pallas import tpu as pltpu
from jax.sharding import Mesh
from jax.sharding import PartitionSpec as P

ITERS = 8
GX = ("gx_0", "gx_1")
GY = ("gy_0", "gy_1", "gy_2")
BX, BY, NZ = 8, 16, 256
H = 8
EX, EY = BX + 2 * H, BY + 2 * H
VMEM = pl.BlockSpec(memory_space=pltpu.VMEM)
SMEM = pl.BlockSpec(memory_space=pltpu.SMEM)


def shift_pairs(n):
    up = [(i, i + 1) for i in range(n - 1)]
    return up, [(b, a) for a, b in up]


def both_ways(array_up, array_down, axes):
    up, down = shift_pairs(lax.axis_size(axes))
    return lax.ppermute(array_up, axes, up), lax.ppermute(array_down, axes, down)


def max_over(value, axes):
    n = lax.axis_size(axes)
    sent = jnp.broadcast_to(value[None], (n, 1, 128))
    return jnp.max(lax.all_to_all(sent, axes, 0, 0, tiled=True), axis=0)


def roll(x, by, axis):
    return pltpu.roll(x, by % x.shape[axis], axis)


def basis(first, second, d, cx, cy, cz, out):
    out[0] = first[H : H + BX, H : H + BY, :]
    bufs = (first, second)
    for k in range(1, ITERS + 1):
        now, nxt = bufs[(k - 1) % 2], bufs[k % 2]

        def row(r, carry, k=k, now=now, nxt=nxt):
            v = now[r]
            y = cy[r]
            z = cz[r]
            a = d[r] * v - cx[r] * now[r + 1] - cx[r - 1] * now[r - 1]
            a = a - y * roll(v, -1, 0) - roll(y * v, 1, 0)
            a = a - z * roll(v, -1, 1) - roll(z * v, 1, 1)
            nxt[r] = 0.5 * a if k == 1 else a - nxt[r]
            return carry

        lax.fori_loop(k, EX - k, row, 0)
        out[k] = nxt[H : H + BX, H : H + BY, :]


def prepare_kernel(keep, own, x_low, x_high, y_low, y_high, d, cx, cy, cz, top, out, shift, first, second):
    for i, ref in enumerate((shift, cx, cy, cz, first)):
        ref[0:H, H : H + BY, :] = x_low[i]
        ref[H : H + BX, H : H + BY, :] = own[i]
        ref[H + BX : EX, H : H + BY, :] = x_high[i]
        ref[:, 0:H, :] = y_low[i]
        ref[:, H + BY : EY, :] = y_high[i]
    lane = lax.broadcasted_iota(jnp.int32, (EY, NZ), 1)
    line = lax.broadcasted_iota(jnp.int32, (EY, NZ), 0)

    def diagonal(r, most):
        y = cy[r]
        z = cz[r]
        total = cx[r] + cx[r - 1] + y + roll(y, 1, 0) + z + jnp.where(lane > 0, roll(z, 1, 1), 0.0)
        diag = shift[r] + total
        d[r] = diag
        return jnp.maximum(most, jnp.where(line > 0, diag + total, 0.0))

    most = lax.fori_loop(1, EX, diagonal, jnp.zeros((EY, NZ), jnp.float32))
    bound = jnp.max(jnp.max(most, axis=0, keepdims=True), axis=1, keepdims=True)
    top[...] = jnp.broadcast_to(bound, top.shape)
    scale = jnp.broadcast_to(4.0 / bound, (1, NZ))
    keep_y = jnp.where(line == H + BY - 1, keep[1], 1.0) * scale
    keep_z = jnp.where(lane == NZ - 1, 0.0, 1.0) * scale

    def rescale(r, carry):
        d[r] = d[r] * scale - 2.0
        cx[r] = cx[r] * (scale * jnp.where(r == H + BX - 1, keep[0], 1.0))
        cy[r] = cy[r] * keep_y
        cz[r] = cz[r] * keep_z
        return carry

    lax.fori_loop(0, EX, rescale, 0)
    basis(first, second, d, cx, cy, cz, out)


def mirror_kernel(own, x_low, x_high, y_low, y_high, d, cx, cy, cz, out, first, second):
    for b, block in enumerate((x_low, own, x_high)):
        for i in range(BX):
            first[b * BX + i, H : H + BY, :] = block[BX - 1 - i]
            first[b * BX + i, 0:H, :] = y_low[b, BX - 1 - i]
            first[b * BX + i, H + BY : EY, :] = y_high[b, BX - 1 - i]
    basis(first, second, d, cx, cy, cz, out)


def polynomials(low, high, bound, top):
    lmin = low * bound
    lmax = high * bound
    theta = (lmax + lmin) / 2.0
    delta = (lmax - lmin) / 2.0
    sigma = theta / delta
    rho = 1.0 / sigma
    half = 0.5 * top
    zero = jnp.zeros_like(bound)
    n = ITERS + 1
    x = [zero] * n
    r = [zero + 1.0] + [zero] * ITERS
    d = [r[0] / theta] + [zero] * ITERS
    for _ in range(ITERS):
        x = [a + b for a, b in zip(x, d)]
        at = d + [zero]
        moved = [0.5 * at[1], at[0] + 0.5 * at[2]] + [0.5 * (at[k - 1] + at[k + 1]) for k in range(2, n)]
        r = [a - half * (b + c) for a, b, c in zip(r, d, moved)]
        rho_new = 1.0 / (2.0 * sigma - rho)
        by, of = rho_new * rho, 2.0 * rho_new / delta
        d = [by * a + of * b for a, b in zip(d, r)]
        rho = rho_new
    return x, r


def combine_kernel(low, high, bound, top, plain, mirrored, pressure, residual):
    found = [polynomials(low[f], high[f], bound[...], top[...]) for f in range(2)]
    sums, gaps = [], []
    for part in range(2):
        sums.append([0.5 * (a + b) for a, b in zip(found[0][part], found[1][part])])
        gaps.append([0.5 * (a - b) for a, b in zip(found[0][part], found[1][part])])
    tiles = [(i, j) for i in range(0, BY, 8) for j in range(0, NZ, 128)]

    def row(r, carry):
        for i, j in tiles:
            p = q = None
            for k in range(ITERS + 1):
                a = plain[k, r, i : i + 8, j : j + 128]
                b = mirrored[k, r, i : i + 8, j : j + 128]
                if k < ITERS:
                    t = sums[0][k] * a + gaps[0][k] * b
                    p = t if p is None else p + t
                t = sums[1][k] * a + gaps[1][k] * b
                q = t if q is None else q + t
            pressure[r, i : i + 8, j : j + 128] = p
            residual[r, i : i + 8, j : j + 128] = q
        return carry

    lax.fori_loop(0, BX, row, 0)


def f32(*shape):
    return jax.ShapeDtypeStruct(shape, jnp.float32)


def shards(right_side, shift, coef_x, coef_y, coef_z, low_frac, high_frac):
    nx, ny = lax.axis_size(GX), lax.axis_size(GY)
    me_x, me_y = lax.axis_index(GX), lax.axis_index(GY)
    up_x, up_y = shift_pairs(nx)[0], shift_pairs(ny)[0]

    before_x = lax.ppermute(coef_x[-1], GX, up_x)
    before_y = lax.ppermute(coef_y[:, -1], GY, up_y)
    own = jnp.stack([shift, coef_x, coef_y, coef_z, right_side])
    x_low, x_high = both_ways(own, own, GX)
    mirror = lax.ppermute(right_side, GX, [(i, nx - 1 - i) for i in range(nx)])

    low_x = jnp.concatenate([before_x[None], coef_x[:-1]], 0)
    low_y = jnp.concatenate([before_y[:, None], coef_y[:, :-1]], 1)
    low_z = jnp.pad(coef_z, ((0, 0), (0, 0), (1, 0)))[:, :, :-1]
    most = jnp.max(shift + 2.0 * (coef_x + low_x + coef_y + low_y + coef_z + low_z))
    bound = max_over(max_over(jnp.full((1, 128), most), GY), GX)
    bound = jnp.broadcast_to(bound, (8, 128))

    sides = jnp.concatenate([x_low, own, x_high], 1)
    y_low, y_high = both_ways(sides[:, :, BY - H :], sides[:, :, :H], GY)
    keep = jnp.stack([me_x < nx - 1, me_y < ny - 1]).astype(jnp.float32)
    wide = f32(EX, EY, NZ)
    scratch = pltpu.VMEM((EX, EY, NZ), jnp.float32)
    basis_out = f32(ITERS + 1, BX, BY, NZ)
    *operator, top, plain = pl.pallas_call(
        prepare_kernel,
        out_shape=(wide, wide, wide, wide, f32(8, 128), basis_out),
        in_specs=[SMEM] + [VMEM] * 5,
        out_specs=(VMEM,) * 6,
        scratch_shapes=[scratch] * 3,
        compiler_params=pltpu.CompilerParams(vmem_limit_bytes=16 << 20),
        cost_estimate=pl.CostEstimate(flops=30_000_000, bytes_accessed=8_000_000, transcendentals=0),
    )(keep, own, x_low, x_high, y_low, y_high)

    m_low, m_high = both_ways(mirror, mirror, GX)
    n_low, n_high = both_ways(
        jnp.stack([a[:, BY - H :] for a in (m_low, mirror, m_high)]),
        jnp.stack([a[:, :H] for a in (m_low, mirror, m_high)]),
        GY,
    )
    mirrored = pl.pallas_call(
        mirror_kernel,
        out_shape=basis_out,
        in_specs=[VMEM] * 9,
        out_specs=VMEM,
        scratch_shapes=[scratch] * 2,
        compiler_params=pltpu.CompilerParams(vmem_limit_bytes=16 << 20),
        cost_estimate=pl.CostEstimate(flops=20_000_000, bytes_accessed=6_000_000, transcendentals=0),
    )(mirror, m_low, m_high, n_low, n_high, *operator)

    return pl.pallas_call(
        combine_kernel,
        out_shape=(f32(BX, BY, NZ), f32(BX, BY, NZ)),
        in_specs=[SMEM, SMEM] + [VMEM] * 4,
        out_specs=(VMEM, VMEM),
        compiler_params=pltpu.CompilerParams(vmem_limit_bytes=8 << 20),
        cost_estimate=pl.CostEstimate(flops=3_000_000, bytes_accessed=3_000_000, transcendentals=0),
    )(low_frac, high_frac, bound, top, plain, mirrored)


def solution(mesh):
    torus = Mesh(mesh.devices.reshape(32, 2, 4, 2, 2), GX + GY)
    block = P(GX, GY, None)
    return jax.shard_map(
        shards,
        mesh=torus,
        in_specs=(block,) * 5 + (P(), P()),
        out_specs=(block, block),
        check_vma=False,
    )
```

```python
import jax
import jax.numpy as jnp
from jax import lax
from jax.experimental import pallas as pl
from jax.experimental.pallas import tpu as pltpu
from jax.sharding import Mesh
from jax.sharding import PartitionSpec as P


ITERS = 8
GX = ("gx_0", "gx_1")
GY = ("gy_0", "gy_1", "gy_2")
BX, BY, NZ = 8, 16, 256
H = 8
PAD = 8
EX, EY = BX + 2 * H, BY + 2 * H
NEAR = ("gx_1",) + GY
VMEM = pl.BlockSpec(memory_space=pltpu.VMEM)
SMEM = pl.BlockSpec(memory_space=pltpu.SMEM)


def shift_pairs(n):
    up = [(i, i + 1) for i in range(n - 1)]
    return up, [(b, a) for a, b in up]


def both_ways(array_up, array_down, axes):
    up, down = shift_pairs(lax.axis_size(axes))
    return lax.ppermute(array_up, axes, up), lax.ppermute(array_down, axes, down)


def turn(x, by):
    return pltpu.roll(x, by % 128, 1)


def basis(first, second, d, cx, cy, ly, cz, lz, out):
    lane = lax.broadcasted_iota(jnp.int32, (8, 128), 1)
    at_start, at_end = lane == 0, lane == 127
    bufs = (first, second)
    for k in range(1, ITERS + 1):
        now, nxt = bufs[(k - 1) % 2], bufs[k % 2]
        for tile in range(EY // 8):
            inner = H <= 8 * tile < H + BY
            start = k if inner else k + 1
            y = PAD + 8 * tile
            if start >= EX - start or (k == ITERS and not inner):
                continue
            below = [now[start - 1, h, y : y + 8, :] for h in range(2)]
            here = [now[start, h, y : y + 8, :] for h in range(2)]
            face = [cx[start - 1, h, y : y + 8, :] for h in range(2)]
            for r in range(start, EX - start):
                above = [now[r + 1, h, y : y + 8, :] for h in range(2)]
                face_up = [cx[r, h, y : y + 8, :] for h in range(2)]
                ahead = [turn(v, -1) for v in here]
                behind = [turn(v, 1) for v in here]
                ahead[0] = jnp.where(at_end, ahead[1], ahead[0])
                behind[1] = jnp.where(at_start, behind[0], behind[1])
                for h in range(2):
                    a = d[r, h, y : y + 8, :] * here[h] - (face_up[h] * above[h] + face[h] * below[h])
                    side = cy[r, h, y : y + 8, :] * now[r, h, y + 1 : y + 9, :]
                    side = side + ly[r, h, y : y + 8, :] * now[r, h, y - 1 : y + 7, :]
                    wall = cz[r, h, y : y + 8, :] * ahead[h] + lz[r, h, y : y + 8, :] * behind[h]
                    a = a - (side + wall)
                    a = 0.5 * a if k == 1 else a - nxt[r, h, y : y + 8, :]
                    nxt[r, h, y : y + 8, :] = a
                    if inner and H <= r < H + BX:
                        out[k, r - H, h, y - PAD - H : y - PAD - H + 8, :] = a
                below, here, face = here, above, face_up
    return out


def place(ref, r, y, value):
    for h in range(2):
        ref[r, h, PAD + y : PAD + y + value.shape[0], :] = value[:, 128 * h : 128 * h + 128]


def prepare_kernel(
    keep, own, x_low, x_high, y_low, y_high, d, cx, cy, ly, cz, lz, top, out, shift, first, second
):
    lane = lax.broadcasted_iota(jnp.int32, (8, 128), 1)
    line = lax.broadcasted_iota(jnp.int32, (8, 128), 0)
    fields = (shift, cx, cy, cz, first)
    for b, block in enumerate((x_low, own, x_high)):

        def assemble(i, carry, b=b, block=block):
            for n, ref in enumerate(fields):
                r = b * BX + i
                place(ref, r, 0, y_low[n, r])
                place(ref, r, H, block[n, i])
                place(ref, r, H + BY, y_high[n, r])
            return carry

        lax.fori_loop(0, BX, assemble, 0)
    for i in range(BX):
        for h in range(2):
            out[0, i, h] = own[4, i, :, 128 * h : 128 * h + 128]

    tiles = [PAD + 8 * t for t in range(EY // 8)]

    def diagonal(r, most):
        for y in tiles:
            z = [cz[r, h, y : y + 8, :] for h in range(2)]
            behind = [turn(v, 1) for v in z]
            behind[1] = jnp.where(lane == 0, behind[0], behind[1])
            behind[0] = jnp.where(lane == 0, 0.0, behind[0])
            for h in range(2):
                lower = cy[r, h, y - 1 : y + 7, :]
                total = cx[r, h, y : y + 8, :] + cx[r - 1, h, y : y + 8, :]
                total = total + cy[r, h, y : y + 8, :] + lower + z[h] + behind[h]
                diag = shift[r, h, y : y + 8, :] + total
                d[r, h, y : y + 8, :] = diag
                ly[r, h, y : y + 8, :] = lower
                lz[r, h, y : y + 8, :] = behind[h]
                row_bound = diag + total
                if y == PAD:
                    row_bound = jnp.where(line > 0, row_bound, 0.0)
                most = jnp.maximum(most, row_bound)
        return most

    most = lax.fori_loop(1, EX, diagonal, jnp.zeros((8, 128), jnp.float32))
    bound = jnp.max(jnp.max(most, axis=0, keepdims=True), axis=1, keepdims=True)
    top[...] = jnp.broadcast_to(bound, top.shape)
    scale = jnp.broadcast_to(4.0 / bound, (8, 128))
    inside = scale * keep[1]

    def rescale(r, carry):
        scale_x = jnp.where(r == H + BX - 1, scale * keep[0], scale)
        for y in tiles:
            last = y - PAD + 8 == H + BY
            after = y - PAD == H + BY
            for h in range(2):
                at = (r, h, slice(y, y + 8), slice(None))
                d[at] = d[at] * scale - 2.0
                cx[at] = cx[at] * scale_x
                cy[at] = cy[at] * (jnp.where(line == 7, inside, scale) if last else scale)
                ly[at] = ly[at] * (jnp.where(line == 0, inside, scale) if after else scale)
                cz[at] = cz[at] * (scale if h == 0 else jnp.where(lane == 127, 0.0, scale))
                lz[at] = lz[at] * scale
        return carry

    lax.fori_loop(0, EX, rescale, 0)
    basis(first, second, d, cx, cy, ly, cz, lz, out)


def mirror_kernel(own, x_low, x_high, y_low, y_high, d, cx, cy, ly, cz, lz, out, first, second):
    for b, block in enumerate((x_low, own, x_high)):
        for i in range(BX):
            r = b * BX + i
            place(first, r, 0, y_low[b * BX + BX - 1 - i])
            place(first, r, H, block[BX - 1 - i])
            place(first, r, H + BY, y_high[b * BX + BX - 1 - i])
    for i in range(BX):
        for h in range(2):
            out[0, i, h] = own[BX - 1 - i, :, 128 * h : 128 * h + 128]
    basis(first, second, d, cx, cy, ly, cz, lz, out)


def pack_kernel(shift, cx, cy, cz, right_side, own, plane_x, plane_y, sems):
    copies = [pltpu.make_async_copy(a, own.at[n], sems.at[n]) for n, a in enumerate((shift, cx, cy, cz, right_side))]
    for copy in copies:
        copy.start()
    copies[1].wait()
    plane_x[...] = own[1, BX - 1]
    copies[2].wait()
    for i in range(BX):
        plane_y[i : i + 1, :] = own[2, i, BY - 1 : BY, :]
    for n in (0, 3, 4):
        copies[n].wait()


def edge_kernel(x_low, own, x_high, first_lines, last_lines):
    for b, block in enumerate((x_low, own, x_high)):
        rows = pl.ds(b * BX, BX)
        if len(block.shape) == 3:
            first_lines[rows] = block[:, :H, :]
            last_lines[rows] = block[:, BY - H :, :]
        else:
            for n in range(block.shape[0]):
                first_lines[n, rows] = block[n, :, :H, :]
                last_lines[n, rows] = block[n, :, BY - H :, :]


def bound_kernel(own, before_x, before_y, out):
    lane = lax.broadcasted_iota(jnp.int32, (BY, NZ), 1)
    line = lax.broadcasted_iota(jnp.int32, (BY, NZ), 0)
    most = jnp.zeros((BY, NZ), jnp.float32)
    for r in range(BX):
        x, y, z = own[1, r], own[2, r], own[3, r]
        low_x = before_x[...] if r == 0 else own[1, r - 1]
        low_y = jnp.where(line == 0, before_y[r : r + 1, :], pltpu.roll(y, 1, 0))
        low_z = jnp.where(lane == 0, 0.0, pltpu.roll(z, 1, 1))
        most = jnp.maximum(most, own[0, r] + 2.0 * (x + low_x + y + low_y + z + low_z))
    most = jnp.max(jnp.max(most, axis=0, keepdims=True), axis=1, keepdims=True)
    out[...] = jnp.broadcast_to(most[None], out.shape)


def spread_kernel(values, out):
    most = values[0]
    for i in range(1, values.shape[0]):
        most = jnp.maximum(most, values[i])
    out[...] = jnp.broadcast_to(most[None], out.shape)


def polynomials(low, high, bound, top):
    lmin = low * bound
    lmax = high * bound
    theta = (lmax + lmin) / 2.0
    delta = (lmax - lmin) / 2.0
    sigma = theta / delta
    rho = 1.0 / sigma
    half = 0.5 * top
    zero = jnp.zeros_like(bound)
    n = ITERS + 1
    x = [zero] * n
    r = [zero + 1.0] + [zero] * ITERS
    d = [r[0] / theta] + [zero] * ITERS
    for _ in range(ITERS):
        x = [a + b for a, b in zip(x, d)]
        at = d + [zero]
        moved = [0.5 * at[1], at[0] + 0.5 * at[2]] + [0.5 * (at[k - 1] + at[k + 1]) for k in range(2, n)]
        r = [a - half * (b + c) for a, b, c in zip(r, d, moved)]
        rho_new = 1.0 / (2.0 * sigma - rho)
        by, of = rho_new * rho, 2.0 * rho_new / delta
        d = [by * a + of * b for a, b in zip(d, r)]
        rho = rho_new
    return x, r


def combine_kernel(low, high, bounds, top, plain, mirrored, pressure, residual):
    bound = bounds[0]
    for i in range(1, bounds.shape[0]):
        bound = jnp.maximum(bound, bounds[i])
    bound = jnp.broadcast_to(bound, (8, 128))
    found = [polynomials(low[f], high[f], bound, top[...]) for f in range(2)]
    sums, gaps = [], []
    for part in range(2):
        sums.append([0.5 * (a + b) for a, b in zip(found[0][part], found[1][part])])
        gaps.append([0.5 * (a - b) for a, b in zip(found[0][part], found[1][part])])

    def row(r, carry):
        for i in range(0, BY, 8):
            for h in range(2):
                p = q = None
                for k in range(ITERS + 1):
                    a = plain[k, r, h, i : i + 8, :]
                    b = mirrored[k, r, h, i : i + 8, :]
                    if k < ITERS:
                        t = sums[0][k] * a + gaps[0][k] * b
                        p = t if p is None else p + t
                    t = sums[1][k] * a + gaps[1][k] * b
                    q = t if q is None else q + t
                pressure[r, i : i + 8, 128 * h : 128 * h + 128] = p
                residual[r, i : i + 8, 128 * h : 128 * h + 128] = q
        return carry

    lax.fori_loop(0, BX, row, 0)


def f32(*shape):
    return jax.ShapeDtypeStruct(shape, jnp.float32)


def kernel(body, out, operands, smem=0, scratch=(), mib=16, flops=1_000_000, where=VMEM):
    nbytes = sum(a.size * 4 for a in operands)
    return pl.pallas_call(
        body,
        out_shape=out,
        in_specs=[SMEM] * smem + [where] * (len(operands) - smem),
        out_specs=jax.tree.map(lambda _: VMEM, out),
        scratch_shapes=scratch,
        compiler_params=pltpu.CompilerParams(vmem_limit_bytes=mib << 20),
        cost_estimate=pl.CostEstimate(flops=flops, bytes_accessed=nbytes, transcendentals=0),
    )(*operands)


def shards(right_side, shift, coef_x, coef_y, coef_z, low_frac, high_frac):
    nx, ny = lax.axis_size(GX), lax.axis_size(GY)
    me_x, me_y = lax.axis_index(GX), lax.axis_index(GY)
    up_x, up_y = shift_pairs(nx)[0], shift_pairs(ny)[0]
    nz_chips, near = lax.axis_size("gx_0"), lax.axis_size(NEAR)

    own, plane_x, plane_y = kernel(
        pack_kernel,
        (f32(5, BX, BY, NZ), f32(BY, NZ), f32(BX, NZ)),
        (shift, coef_x, coef_y, coef_z, right_side),
        scratch=[pltpu.SemaphoreType.DMA((5,))],
        where=pl.BlockSpec(memory_space=pl.ANY),
        mib=56,
    )
    before_x = lax.ppermute(plane_x, GX, up_x)
    before_y = lax.ppermute(plane_y, GY, up_y)
    x_low, x_high = both_ways(own, own, GX)
    mirror = lax.ppermute(right_side, GX, [(i, nx - 1 - i) for i in range(nx)])

    most = kernel(bound_kernel, f32(near, 1, 128), (own, before_x, before_y), mib=4)
    most = lax.all_to_all(most, NEAR, 0, 0, tiled=True)
    most = kernel(spread_kernel, f32(nz_chips, 1, 128), (most,), mib=4)
    bounds = lax.all_to_all(most, "gx_0", 0, 0, tiled=True)

    edge = f32(5, EX, H, NZ)
    first_lines, last_lines = kernel(edge_kernel, (edge, edge), (x_low, own, x_high))
    y_low, y_high = both_ways(last_lines, first_lines, GY)
    keep = jnp.stack([me_x < nx - 1, me_y < ny - 1]).astype(jnp.float32)
    wide = f32(EX, 2, EY + 2 * PAD, 128)
    scratch = pltpu.VMEM(wide.shape, jnp.float32)
    basis_out = f32(ITERS + 1, BX, 2, BY, 128)
    *operator, top, plain = kernel(
        prepare_kernel,
        (wide,) * 6 + (f32(8, 128), basis_out),
        (keep, own, x_low, x_high, y_low, y_high),
        smem=1,
        scratch=[scratch] * 3,
        flops=30_000_000,
    )

    m_low, m_high = both_ways(mirror, mirror, GX)
    edge = f32(EX, H, NZ)
    first_lines, last_lines = kernel(edge_kernel, (edge, edge), (m_low, mirror, m_high), mib=8)
    n_low, n_high = both_ways(last_lines, first_lines, GY)
    mirrored = kernel(
        mirror_kernel,
        basis_out,
        (mirror, m_low, m_high, n_low, n_high, *operator),
        scratch=[scratch] * 2,
        flops=20_000_000,
    )
    return kernel(
        combine_kernel,
        (f32(BX, BY, NZ), f32(BX, BY, NZ)),
        (low_frac, high_frac, bounds, top, plain, mirrored),
        smem=2,
        mib=8,
        flops=3_000_000,
    )


def solution(mesh):
    torus = Mesh(mesh.devices.reshape(32, 2, 4, 2, 2), GX + GY)
    block = P(GX, GY, None)
    return jax.shard_map(
        shards,
        mesh=torus,
        in_specs=(block,) * 5 + (P(), P()),
        out_specs=(block, block),
        check_vma=False,
    )
```

```python
import jax
import jax.numpy as jnp
from jax import lax
from jax.experimental import pallas as pl
from jax.experimental.pallas import tpu as pltpu
from jax.sharding import Mesh
from jax.sharding import PartitionSpec as P


ITERS = 8
GX = ("gx_0", "gx_1")
GY = ("gy_0", "gy_1", "gy_2")
BX, BY, NZ = 8, 16, 256
H = 8
PAD = 8
EX, EY = BX + 2 * H, BY + 2 * H
NEAR = ("gx_1",) + GY
VMEM = pl.BlockSpec(memory_space=pltpu.VMEM)
SMEM = pl.BlockSpec(memory_space=pltpu.SMEM)
STRIDES = (16, 8, 4, 2, 1)
SHARED = ((7, 1, 1), (6, 2, 2), (5, 3, 3), (16, 22, 1), (17, 21, 2), (18, 20, 3), (4, 19, 4))
EDGE = BX + len(SHARED)


def shift_pairs(n):
    up = [(i, i + 1) for i in range(n - 1)]
    return up, [(b, a) for a, b in up]


def both_ways(array_up, array_down, axes):
    up, down = shift_pairs(lax.axis_size(axes))
    return lax.ppermute(array_up, axes, up), lax.ppermute(array_down, axes, down)


def turn(x, by):
    return pltpu.roll(x, by % 128, 1)


def basis(first, second, d, cx, cy, ly, cz, lz, out):
    lane = lax.broadcasted_iota(jnp.int32, (8, 128), 1)
    at_start, at_end = lane == 0, lane == 127
    bufs = (first, second)
    for k in range(1, ITERS + 1):
        now, nxt = bufs[(k - 1) % 2], bufs[k % 2]
        for tile in range(EY // 8):
            inner = H <= 8 * tile < H + BY
            start = k if inner else k + 1
            y = PAD + 8 * tile
            if start >= EX - start or (k == ITERS and not inner):
                continue
            below = [now[start - 1, h, y : y + 8, :] for h in range(2)]
            here = [now[start, h, y : y + 8, :] for h in range(2)]
            face = [cx[start - 1, h, y : y + 8, :] for h in range(2)]
            for r in range(start, EX - start):
                above = [now[r + 1, h, y : y + 8, :] for h in range(2)]
                face_up = [cx[r, h, y : y + 8, :] for h in range(2)]
                ahead = [turn(v, -1) for v in here]
                behind = [turn(v, 1) for v in here]
                ahead[0] = jnp.where(at_end, ahead[1], ahead[0])
                behind[1] = jnp.where(at_start, behind[0], behind[1])
                for h in range(2):
                    a = d[r, h, y : y + 8, :] * here[h] - (face_up[h] * above[h] + face[h] * below[h])
                    side = cy[r, h, y : y + 8, :] * now[r, h, y + 1 : y + 9, :]
                    side = side + ly[r, h, y : y + 8, :] * now[r, h, y - 1 : y + 7, :]
                    wall = cz[r, h, y : y + 8, :] * ahead[h] + lz[r, h, y : y + 8, :] * behind[h]
                    a = a - (side + wall)
                    a = 0.5 * a if k == 1 else a - nxt[r, h, y : y + 8, :]
                    nxt[r, h, y : y + 8, :] = a
                    if inner and H <= r < H + BX:
                        out[k, r - H, h, y - PAD - H : y - PAD - H + 8, :] = a
                below, here, face = here, above, face_up
    return out


def place(ref, r, y, value):
    for h in range(2):
        ref[r, h, PAD + y : PAD + y + value.shape[0], :] = value[:, 128 * h : 128 * h + 128]


def place_sides(ref, low, high):
    for i in range(BX):
        place(ref, H + i, 0, low[i])
        place(ref, H + i, H + BY, high[i])
    for t, (a, b, n) in enumerate(SHARED, BX):
        for r, by in ((a, 0), (b, n)):
            at_low, at_high = low[t], high[t]
            if by:
                at_low, at_high = pltpu.roll(at_low, 8 - by, 0), pltpu.roll(at_high, by, 0)
            for row in {1: (0, 1), 22: (22, 23)}.get(r, (r,)):
                place(ref, row, 0, at_low)
                place(ref, row, H + BY, at_high)


def prepare_kernel(
    keep, s_own, x_own, y_own, z_own, b_own, x_low, x_high, y_low, y_high, d, cx, cy, ly, cz, lz, top, out, shift, first, second
):
    lane = lax.broadcasted_iota(jnp.int32, (8, 128), 1)
    line = lax.broadcasted_iota(jnp.int32, (8, 128), 0)
    fields = ((shift, s_own), (cx, x_own), (cy, y_own), (cz, z_own), (first, b_own))
    for n, (ref, own) in enumerate(fields):
        for i in range(BX):
            place(ref, i, H, x_low[n, i])
            place(ref, H + i, H, own[i])
            place(ref, H + BX + i, H, x_high[n, i])
        place_sides(ref, y_low.at[n], y_high.at[n])
    for i in range(BX):
        for h in range(2):
            out[0, i, h] = b_own[i, :, 128 * h : 128 * h + 128]

    tiles = [PAD + 8 * t for t in range(EY // 8)]

    def diagonal(r, most):
        away = jnp.maximum(jnp.maximum(H - r, r - (H + BX - 1)), 0)
        for y in tiles:
            z = [cz[r, h, y : y + 8, :] for h in range(2)]
            behind = [turn(v, 1) for v in z]
            behind[1] = jnp.where(lane == 0, behind[0], behind[1])
            behind[0] = jnp.where(lane == 0, 0.0, behind[0])
            for h in range(2):
                lower = cy[r, h, y - 1 : y + 7, :]
                total = cx[r, h, y : y + 8, :] + cx[r - 1, h, y : y + 8, :]
                total = total + cy[r, h, y : y + 8, :] + lower + z[h] + behind[h]
                diag = shift[r, h, y : y + 8, :] + total
                d[r, h, y : y + 8, :] = diag
                ly[r, h, y : y + 8, :] = lower
                lz[r, h, y : y + 8, :] = behind[h]
                row_bound = diag + total
                if y == tiles[0]:
                    row_bound = jnp.where(line > away, row_bound, 0.0)
                if y == tiles[-1]:
                    row_bound = jnp.where(line < 7 - away, row_bound, 0.0)
                most = jnp.maximum(most, row_bound)
        return most

    most = lax.fori_loop(1, EX - 1, diagonal, jnp.zeros((8, 128), jnp.float32))
    bound = jnp.max(jnp.max(most, axis=0, keepdims=True), axis=1, keepdims=True)
    top[...] = jnp.broadcast_to(bound, top.shape)
    scale = jnp.broadcast_to(4.0 / bound, (8, 128))
    inside = scale * keep[1]

    def rescale(r, carry):
        scale_x = jnp.where(r == H + BX - 1, scale * keep[0], scale)
        for y in tiles:
            last = y - PAD + 8 == H + BY
            after = y - PAD == H + BY
            for h in range(2):
                at = (r, h, slice(y, y + 8), slice(None))
                d[at] = d[at] * scale - 2.0
                cx[at] = cx[at] * scale_x
                cy[at] = cy[at] * (jnp.where(line == 7, inside, scale) if last else scale)
                ly[at] = ly[at] * (jnp.where(line == 0, inside, scale) if after else scale)
                cz[at] = cz[at] * (scale if h == 0 else jnp.where(lane == 127, 0.0, scale))
                lz[at] = lz[at] * scale
        return carry

    lax.fori_loop(0, EX, rescale, 0)
    basis(first, second, d, cx, cy, ly, cz, lz, out)


def mirror_kernel(own, x_low, x_high, y_low, y_high, d, cx, cy, ly, cz, lz, out, first, second):
    for b, block in enumerate((x_low, own, x_high)):
        for i in range(BX):
            place(first, b * BX + i, H, block[BX - 1 - i])
    place_sides(first, y_low, y_high)
    for i in range(BX):
        for h in range(2):
            out[0, i, h] = own[BX - 1 - i, :, 128 * h : 128 * h + 128]
    basis(first, second, d, cx, cy, ly, cz, lz, out)


def pack_kernel(shift, cx, cy, cz, right_side, own, plane_x, plane_y, sems):
    copies = [pltpu.make_async_copy(a, own.at[n], sems.at[n]) for n, a in enumerate((shift, cx, cy, cz, right_side))]
    for copy in copies:
        copy.start()
    copies[1].wait()
    plane_x[...] = own[1, BX - 1]
    copies[2].wait()
    for i in range(BX):
        plane_y[i : i + 1, :] = own[2, i, BY - 1 : BY, :]
    for n in (0, 3, 4):
        copies[n].wait()


def edges(row, first_lines, last_lines):
    line = lax.broadcasted_iota(jnp.int32, (H, NZ), 0)
    for i in range(BX):
        first_lines[i] = row(H + i, 0)
        last_lines[i] = row(H + i, BY - H)
    for t, (a, b, n) in enumerate(SHARED, BX):
        last_lines[t] = jnp.where(line >= n, row(a, BY - H), pltpu.roll(row(b, BY - H), n, 0))
        first_lines[t] = jnp.where(line < H - n, row(a, 0), pltpu.roll(row(b, 0), H - n, 0))


def edge_kernel(s_own, x_own, y_own, z_own, b_own, x_low, x_high, first_lines, last_lines):
    for n, own in enumerate((s_own, x_own, y_own, z_own, b_own)):

        def row(r, y, n=n, own=own):
            block = (x_low.at[n], own, x_high.at[n])[r // BX]
            return block[r % BX, y : y + H, :]

        edges(row, first_lines.at[n], last_lines.at[n])


def mirror_edge_kernel(own, x_low, x_high, first_lines, last_lines):
    edges(lambda r, y: (x_low, own, x_high)[r // BX][BX - 1 - r % BX, y : y + H, :], first_lines, last_lines)


def bound_kernel(shift, cx, cy, cz, before_x, before_y, out):
    lane = lax.broadcasted_iota(jnp.int32, (BY, NZ), 1)
    line = lax.broadcasted_iota(jnp.int32, (BY, NZ), 0)
    most = jnp.zeros((BY, NZ), jnp.float32)
    for r in range(BX):
        x, y, z = cx[r], cy[r], cz[r]
        low_x = before_x[...] if r == 0 else cx[r - 1]
        low_y = jnp.where(line == 0, before_y[r : r + 1, :], pltpu.roll(y, 1, 0))
        low_z = jnp.where(lane == 0, 0.0, pltpu.roll(z, 1, 1))
        most = jnp.maximum(most, shift[r] + 2.0 * (x + low_x + y + low_y + z + low_z))
    most = jnp.max(jnp.max(most, axis=0, keepdims=True), axis=1, keepdims=True)
    out[...] = jnp.broadcast_to(most[None], out.shape)


def spread_kernel(values, out):
    most = values[0]
    for i in range(1, values.shape[0]):
        most = jnp.maximum(most, values[i])
    out[...] = jnp.broadcast_to(most, out.shape)


def polynomials(low, high, bound, top):
    lmin = low * bound
    lmax = high * bound
    theta = (lmax + lmin) / 2.0
    delta = (lmax - lmin) / 2.0
    sigma = theta / delta
    rho = 1.0 / sigma
    half = 0.5 * top
    zero = jnp.zeros_like(bound)
    n = ITERS + 1
    x = [zero] * n
    r = [zero + 1.0] + [zero] * ITERS
    d = [r[0] / theta] + [zero] * ITERS
    for _ in range(ITERS):
        x = [a + b for a, b in zip(x, d)]
        at = d + [zero]
        moved = [0.5 * at[1], at[0] + 0.5 * at[2]] + [0.5 * (at[k - 1] + at[k + 1]) for k in range(2, n)]
        r = [a - half * (b + c) for a, b, c in zip(r, d, moved)]
        rho_new = 1.0 / (2.0 * sigma - rho)
        by, of = rho_new * rho, 2.0 * rho_new / delta
        d = [by * a + of * b for a, b in zip(d, r)]
        rho = rho_new
    return x, r


def combine_kernel(low, high, bound, other_bound, top, plain, mirrored, pressure, residual):
    bound = jnp.maximum(bound[...], other_bound[...])
    found = [polynomials(low[f], high[f], bound, top[...]) for f in range(2)]
    sums, gaps = [], []
    for part in range(2):
        sums.append([0.5 * (a + b) for a, b in zip(found[0][part], found[1][part])])
        gaps.append([0.5 * (a - b) for a, b in zip(found[0][part], found[1][part])])

    def row(r, carry):
        for i in range(0, BY, 8):
            for h in range(2):
                p = q = None
                for k in range(ITERS + 1):
                    a = plain[k, r, h, i : i + 8, :]
                    b = mirrored[k, r, h, i : i + 8, :]
                    if k < ITERS:
                        t = sums[0][k] * a + gaps[0][k] * b
                        p = t if p is None else p + t
                    t = sums[1][k] * a + gaps[1][k] * b
                    q = t if q is None else q + t
                pressure[r, i : i + 8, 128 * h : 128 * h + 128] = p
                residual[r, i : i + 8, 128 * h : 128 * h + 128] = q
        return carry

    lax.fori_loop(0, BX, row, 0)


def f32(*shape):
    return jax.ShapeDtypeStruct(shape, jnp.float32)


def kernel(body, out, operands, smem=0, scratch=(), mib=16, flops=1_000_000, where=VMEM):
    nbytes = sum(a.size * 4 for a in operands)
    return pl.pallas_call(
        body,
        out_shape=out,
        in_specs=[SMEM] * smem + [where] * (len(operands) - smem),
        out_specs=jax.tree.map(lambda _: VMEM, out),
        scratch_shapes=scratch,
        compiler_params=pltpu.CompilerParams(vmem_limit_bytes=mib << 20),
        cost_estimate=pl.CostEstimate(flops=flops, bytes_accessed=nbytes, transcendentals=0),
    )(*operands)


def shards(right_side, shift, coef_x, coef_y, coef_z, low_frac, high_frac):
    nx, ny = lax.axis_size(GX), lax.axis_size(GY)
    me_x, me_y = lax.axis_index(GX), lax.axis_index(GY)
    up_x, up_y = shift_pairs(nx)[0], shift_pairs(ny)[0]
    near = lax.axis_size(NEAR)
    given = (shift, coef_x, coef_y, coef_z, right_side)

    mirror = lax.ppermute(right_side, GX, [(i, nx - 1 - i) for i in range(nx)])
    own, plane_x, plane_y = kernel(
        pack_kernel,
        (f32(5, BX, BY, NZ), f32(BY, NZ), f32(BX, NZ)),
        given,
        scratch=[pltpu.SemaphoreType.DMA((5,))],
        where=pl.BlockSpec(memory_space=pl.ANY),
        mib=56,
    )
    x_low, x_high = both_ways(own, own, GX)
    before_x = lax.ppermute(plane_x, GX, up_x)
    before_y = lax.ppermute(plane_y, GY, up_y)

    most = kernel(bound_kernel, f32(near, 1, 128), (*given[:4], before_x, before_y), mib=2)
    most = lax.all_to_all(most, NEAR, 0, 0, tiled=True)
    most = kernel(spread_kernel, f32(8, 128), (most,), mib=2)
    other = most
    for stride in STRIDES:
        most = jnp.maximum(most, other)
        other = lax.ppermute(most, "gx_0", [(i, i ^ stride) for i in range(lax.axis_size("gx_0"))])

    edge = f32(5, EDGE, H, NZ)
    first_lines, last_lines = kernel(edge_kernel, (edge, edge), (*given, x_low, x_high), mib=2)
    y_low, y_high = both_ways(last_lines, first_lines, GY)
    keep = jnp.stack([me_x < nx - 1, me_y < ny - 1]).astype(jnp.float32)
    wide = f32(EX, 2, EY + 2 * PAD, 128)
    scratch = pltpu.VMEM(wide.shape, jnp.float32)
    basis_out = f32(ITERS + 1, BX, 2, BY, 128)
    *operator, top, plain = kernel(
        prepare_kernel,
        (wide,) * 6 + (f32(8, 128), basis_out),
        (keep, *given, x_low, x_high, y_low, y_high),
        smem=1,
        scratch=[scratch] * 3,
        flops=30_000_000,
        mib=6,
    )

    m_low, m_high = both_ways(mirror, mirror, GX)
    edge = f32(EDGE, H, NZ)
    first_lines, last_lines = kernel(mirror_edge_kernel, (edge, edge), (mirror, m_low, m_high), mib=2)
    n_low, n_high = both_ways(last_lines, first_lines, GY)
    mirrored = kernel(
        mirror_kernel,
        basis_out,
        (mirror, m_low, m_high, n_low, n_high, *operator),
        scratch=[scratch] * 2,
        flops=20_000_000,
        mib=4,
    )
    return kernel(
        combine_kernel,
        (f32(BX, BY, NZ), f32(BX, BY, NZ)),
        (low_frac, high_frac, most, other, top, plain, mirrored),
        smem=2,
        mib=2,
        flops=3_000_000,
    )


def solution(mesh):
    torus = Mesh(mesh.devices.reshape(32, 2, 4, 2, 2), GX + GY)
    block = P(GX, GY, None)
    return jax.shard_map(
        shards,
        mesh=torus,
        in_specs=(block,) * 5 + (P(), P()),
        out_specs=(block, block),
        check_vma=False,
    )
```

```python
import jax
import jax.numpy as jnp
from jax import lax
from jax.experimental import pallas as pl
from jax.experimental.pallas import tpu as pltpu
from jax.sharding import Mesh
from jax.sharding import PartitionSpec as P


ITERS = 8
GX = ("gx_0", "gx_1")
GY = ("gy_0", "gy_1", "gy_2")
BX, BY, NZ = 8, 16, 256
H = 8
PAD = 8
EX, EY = BX + 2 * H, BY + 2 * H
NEAR = ("gx_1",) + GY
VMEM = pl.BlockSpec(memory_space=pltpu.VMEM)
SMEM = pl.BlockSpec(memory_space=pltpu.SMEM)
ANY = pl.BlockSpec(memory_space=pl.ANY)
SHARED = ((7, 1, 1), (6, 2, 2), (5, 3, 3), (16, 22, 1), (17, 21, 2), (18, 20, 3), (4, 19, 4))
EDGE = BX + len(SHARED)


def shift_pairs(n):
    up = [(i, i + 1) for i in range(n - 1)]
    return up, [(b, a) for a, b in up]


def both_ways(array_up, array_down, axes):
    up, down = shift_pairs(lax.axis_size(axes))
    return lax.ppermute(array_up, axes, up), lax.ppermute(array_down, axes, down)


def turn(x, by):
    return pltpu.roll(x, by % 128, 1)


def basis(first, second, d, cx, cy, ly, cz, lz, out):
    lane = lax.broadcasted_iota(jnp.int32, (8, 128), 1)
    at_start, at_end = lane == 0, lane == 127
    bufs = (first, second)
    for k in range(1, ITERS + 1):
        now, nxt = bufs[(k - 1) % 2], bufs[k % 2]
        for tile in range(EY // 8):
            inner = H <= 8 * tile < H + BY
            start = k if inner else k + 1
            y = PAD + 8 * tile
            if start >= EX - start or (k == ITERS and not inner):
                continue
            below = [now[start - 1, h, y : y + 8, :] for h in range(2)]
            here = [now[start, h, y : y + 8, :] for h in range(2)]
            face = [cx[start - 1, h, y : y + 8, :] for h in range(2)]
            for r in range(start, EX - start):
                above = [now[r + 1, h, y : y + 8, :] for h in range(2)]
                face_up = [cx[r, h, y : y + 8, :] for h in range(2)]
                ahead = [turn(v, -1) for v in here]
                behind = [turn(v, 1) for v in here]
                ahead[0] = jnp.where(at_end, ahead[1], ahead[0])
                behind[1] = jnp.where(at_start, behind[0], behind[1])
                for h in range(2):
                    a = d[r, h, y : y + 8, :] * here[h] - (face_up[h] * above[h] + face[h] * below[h])
                    side = cy[r, h, y : y + 8, :] * now[r, h, y + 1 : y + 9, :]
                    side = side + ly[r, h, y : y + 8, :] * now[r, h, y - 1 : y + 7, :]
                    wall = cz[r, h, y : y + 8, :] * ahead[h] + lz[r, h, y : y + 8, :] * behind[h]
                    a = a - (side + wall)
                    a = 0.5 * a if k == 1 else a - nxt[r, h, y : y + 8, :]
                    nxt[r, h, y : y + 8, :] = a
                    if inner and H <= r < H + BX:
                        out[k, r - H, h, y - PAD - H : y - PAD - H + 8, :] = a
                below, here, face = here, above, face_up
    return out


def place(ref, r, y, value):
    for h in range(2):
        ref[r, h, PAD + y : PAD + y + value.shape[0], :] = value[:, 128 * h : 128 * h + 128]


def place_sides(ref, low, high):
    for i in range(BX):
        place(ref, H + i, 0, low[i])
        place(ref, H + i, H + BY, high[i])
    for t, (a, b, n) in enumerate(SHARED, BX):
        for r, by in ((a, 0), (b, n)):
            at_low, at_high = low[t], high[t]
            if by:
                at_low, at_high = pltpu.roll(at_low, 8 - by, 0), pltpu.roll(at_high, by, 0)
            for row in {1: (0, 1), 22: (22, 23)}.get(r, (r,)):
                place(ref, row, 0, at_low)
                place(ref, row, H + BY, at_high)


def prepare_kernel(
    own, x_low, x_high, y_low, y_high, d, cx, cy, ly, cz, lz, top, out, shift, first, second, held, sem
):
    lane = lax.broadcasted_iota(jnp.int32, (8, 128), 1)
    line = lax.broadcasted_iota(jnp.int32, (8, 128), 0)
    keep = [jnp.where(lax.axis_index(axes) < lax.axis_size(axes) - 1, 1.0, 0.0) for axes in (GX, GY)]
    copy = pltpu.make_async_copy(own, held, sem)
    copy.start()
    fields = (shift, cx, cy, cz, first)
    for n, ref in enumerate(fields):
        for i in range(BX):
            place(ref, i, H, x_low[n, i])
            place(ref, H + BX + i, H, x_high[n, i])
        place_sides(ref, y_low.at[n], y_high.at[n])
    copy.wait()
    for n, ref in enumerate(fields):
        for i in range(BX):
            place(ref, H + i, H, held[n, i])
    for i in range(BX):
        for h in range(2):
            out[0, i, h] = held[4, i, :, 128 * h : 128 * h + 128]

    tiles = [PAD + 8 * t for t in range(EY // 8)]

    def diagonal(r, most):
        away = jnp.maximum(jnp.maximum(H - r, r - (H + BX - 1)), 0)
        for y in tiles:
            z = [cz[r, h, y : y + 8, :] for h in range(2)]
            behind = [turn(v, 1) for v in z]
            behind[1] = jnp.where(lane == 0, behind[0], behind[1])
            behind[0] = jnp.where(lane == 0, 0.0, behind[0])
            for h in range(2):
                lower = cy[r, h, y - 1 : y + 7, :]
                total = cx[r, h, y : y + 8, :] + cx[r - 1, h, y : y + 8, :]
                total = total + cy[r, h, y : y + 8, :] + lower + z[h] + behind[h]
                diag = shift[r, h, y : y + 8, :] + total
                d[r, h, y : y + 8, :] = diag
                ly[r, h, y : y + 8, :] = lower
                lz[r, h, y : y + 8, :] = behind[h]
                row_bound = diag + total
                if y == tiles[0]:
                    row_bound = jnp.where(line > away, row_bound, 0.0)
                if y == tiles[-1]:
                    row_bound = jnp.where(line < 7 - away, row_bound, 0.0)
                most = jnp.maximum(most, row_bound)
        return most

    most = lax.fori_loop(1, EX - 1, diagonal, jnp.zeros((8, 128), jnp.float32))
    bound = jnp.max(jnp.max(most, axis=0, keepdims=True), axis=1, keepdims=True)
    top[...] = jnp.broadcast_to(bound, top.shape)
    scale = jnp.broadcast_to(4.0 / bound, (8, 128))
    inside = scale * keep[1]

    def rescale(r, carry):
        scale_x = jnp.where(r == H + BX - 1, scale * keep[0], scale)
        for y in tiles:
            last = y - PAD + 8 == H + BY
            after = y - PAD == H + BY
            for h in range(2):
                at = (r, h, slice(y, y + 8), slice(None))
                d[at] = d[at] * scale - 2.0
                cx[at] = cx[at] * scale_x
                cy[at] = cy[at] * (jnp.where(line == 7, inside, scale) if last else scale)
                ly[at] = ly[at] * (jnp.where(line == 0, inside, scale) if after else scale)
                cz[at] = cz[at] * (scale if h == 0 else jnp.where(lane == 127, 0.0, scale))
                lz[at] = lz[at] * scale
        return carry

    lax.fori_loop(0, EX, rescale, 0)
    basis(first, second, d, cx, cy, ly, cz, lz, out)


def mirror_kernel(own, x_low, x_high, y_low, y_high, d, cx, cy, ly, cz, lz, out, first, second):
    for b, block in enumerate((x_low, own, x_high)):
        for i in range(BX):
            place(first, b * BX + i, H, block[BX - 1 - i])
    place_sides(first, y_low, y_high)
    for i in range(BX):
        for h in range(2):
            out[0, i, h] = own[BX - 1 - i, :, 128 * h : 128 * h + 128]
    basis(first, second, d, cx, cy, ly, cz, lz, out)


def pack_kernel(shift, cx, cy, cz, right_side, own, plane_x, plane_y, most, base_x, base_y, sems):
    copies = [pltpu.make_async_copy(a, own.at[n], sems.at[n]) for n, a in enumerate((shift, cx, cy, cz, right_side))]
    for copy in copies:
        copy.start()
    lane = lax.broadcasted_iota(jnp.int32, (BY, NZ), 1)
    line = lax.broadcasted_iota(jnp.int32, (BY, NZ), 0)
    copies[1].wait()
    plane_x[...] = own[1, BX - 1]
    copies[2].wait()
    for i in range(BX):
        plane_y[i : i + 1, :] = own[2, i, BY - 1 : BY, :]
    copies[0].wait()
    copies[3].wait()
    whole = jnp.zeros((BY, NZ), jnp.float32)
    for r in range(BX):
        x, y, z = own[1, r], own[2, r], own[3, r]
        if r:
            x = x + own[1, r - 1]
        y = y + jnp.where(line == 0, 0.0, pltpu.roll(y, 1, 0))
        z = z + jnp.where(lane == 0, 0.0, pltpu.roll(z, 1, 1))
        row = own[0, r] + 2.0 * (x + y + z)
        base_y[r : r + 1, :] = row[0:1, :]
        if r:
            whole = jnp.maximum(whole, jnp.where(line == 0, 0.0, row))
        else:
            base_x[...] = row
    most[...] = whole
    copies[4].wait()


def edges(row, first_lines, last_lines):
    line = lax.broadcasted_iota(jnp.int32, (H, NZ), 0)
    for i in range(BX):
        first_lines[i] = row(H + i, 0)
        last_lines[i] = row(H + i, BY - H)
    for t, (a, b, n) in enumerate(SHARED, BX):
        last_lines[t] = jnp.where(line >= n, row(a, BY - H), pltpu.roll(row(b, BY - H), n, 0))
        first_lines[t] = jnp.where(line < H - n, row(a, 0), pltpu.roll(row(b, 0), H - n, 0))


def edge_kernel(own, x_low, x_high, first_lines, last_lines, held, sem):
    copy = pltpu.make_async_copy(own, held, sem)
    copy.start()
    copy.wait()
    for n in range(5):

        def row(r, y, n=n):
            return (x_low, held, x_high)[r // BX][n, r % BX, y : y + H, :]

        edges(row, first_lines.at[n], last_lines.at[n])


def mirror_edge_kernel(own, x_low, x_high, first_lines, last_lines):
    edges(lambda r, y: (x_low, own, x_high)[r // BX][BX - 1 - r % BX, y : y + H, :], first_lines, last_lines)


def bound_kernel(most, base_x, base_y, before_x, before_y, out):
    line = lax.broadcasted_iota(jnp.int32, (BY, NZ), 0)
    row = lax.broadcasted_iota(jnp.int32, (BX, NZ), 0)
    corner = jnp.where(line == 0, before_y[0:1, :], 0.0)
    largest = jnp.maximum(most[...], base_x[...] + 2.0 * (before_x[...] + corner))
    first = jnp.where(row == 0, 0.0, base_y[...] + 2.0 * before_y[...])
    largest = jnp.maximum(jnp.max(largest, axis=0, keepdims=True), jnp.max(first, axis=0, keepdims=True))
    largest = jnp.max(largest, axis=1, keepdims=True)
    out[...] = jnp.broadcast_to(largest[None], out.shape)


def spread_kernel(values, out):
    most = values[0]
    for i in range(1, values.shape[0]):
        most = jnp.maximum(most, values[i])
    out[...] = jnp.broadcast_to(most[None], out.shape)


def polynomials(low, high, bound, top):
    lmin = low * bound
    lmax = high * bound
    theta = (lmax + lmin) / 2.0
    delta = (lmax - lmin) / 2.0
    sigma = theta / delta
    rho = 1.0 / sigma
    half = 0.5 * top
    zero = jnp.zeros_like(bound)
    n = ITERS + 1
    x = [zero] * n
    r = [zero + 1.0] + [zero] * ITERS
    d = [r[0] / theta] + [zero] * ITERS
    for _ in range(ITERS):
        x = [a + b for a, b in zip(x, d)]
        at = d + [zero]
        moved = [0.5 * at[1], at[0] + 0.5 * at[2]] + [0.5 * (at[k - 1] + at[k + 1]) for k in range(2, n)]
        r = [a - half * (b + c) for a, b, c in zip(r, d, moved)]
        rho_new = 1.0 / (2.0 * sigma - rho)
        by, of = rho_new * rho, 2.0 * rho_new / delta
        d = [by * a + of * b for a, b in zip(d, r)]
        rho = rho_new
    return x, r


def combine_kernel(low, high, bounds, top, plain, mirrored, pressure, residual):
    bound = bounds[0]
    for i in range(1, bounds.shape[0]):
        bound = jnp.maximum(bound, bounds[i])
    bound = jnp.broadcast_to(bound, (8, 128))
    found = [polynomials(low[f], high[f], bound, top[...]) for f in range(2)]
    sums, gaps = [], []
    for part in range(2):
        sums.append([0.5 * (a + b) for a, b in zip(found[0][part], found[1][part])])
        gaps.append([0.5 * (a - b) for a, b in zip(found[0][part], found[1][part])])

    def row(r, carry):
        for i in range(0, BY, 8):
            for h in range(2):
                p = q = None
                for k in range(ITERS + 1):
                    a = plain[k, r, h, i : i + 8, :]
                    b = mirrored[k, r, h, i : i + 8, :]
                    if k < ITERS:
                        t = sums[0][k] * a + gaps[0][k] * b
                        p = t if p is None else p + t
                    t = sums[1][k] * a + gaps[1][k] * b
                    q = t if q is None else q + t
                pressure[r, i : i + 8, 128 * h : 128 * h + 128] = p
                residual[r, i : i + 8, 128 * h : 128 * h + 128] = q
        return carry

    lax.fori_loop(0, BX, row, 0)


def f32(*shape):
    return jax.ShapeDtypeStruct(shape, jnp.float32)


def kernel(body, out, operands, smem=0, anywhere=0, scratch=(), mib=16, flops=1_000_000):
    nbytes = sum(a.size * 4 for a in operands)
    return pl.pallas_call(
        body,
        out_shape=out,
        in_specs=[SMEM] * smem + [ANY] * anywhere + [VMEM] * (len(operands) - smem - anywhere),
        out_specs=jax.tree.map(lambda _: VMEM, out),
        scratch_shapes=scratch,
        compiler_params=pltpu.CompilerParams(vmem_limit_bytes=mib << 20),
        cost_estimate=pl.CostEstimate(flops=flops, bytes_accessed=nbytes, transcendentals=0),
    )(*operands)


def shards(right_side, shift, coef_x, coef_y, coef_z, low_frac, high_frac):
    nx, ny = lax.axis_size(GX), lax.axis_size(GY)
    up_x, up_y = shift_pairs(nx)[0], shift_pairs(ny)[0]
    near = lax.axis_size(NEAR)
    given = (shift, coef_x, coef_y, coef_z, right_side)

    own, plane_x, plane_y, most, base_x, base_y = kernel(
        pack_kernel,
        (f32(5, BX, BY, NZ), f32(BY, NZ), f32(BX, NZ), f32(BY, NZ), f32(BY, NZ), f32(BX, NZ)),
        given,
        scratch=[pltpu.SemaphoreType.DMA((5,))],
        anywhere=5,
        mib=56,
    )
    before_x = lax.ppermute(plane_x, GX, up_x)
    before_y = lax.ppermute(plane_y, GY, up_y)
    x_low, x_high = both_ways(own, own, GX)
    mirror = lax.ppermute(right_side, GX, [(i, nx - 1 - i) for i in range(nx)])

    most = kernel(bound_kernel, f32(near, 1, 128), (most, base_x, base_y, before_x, before_y), mib=2)
    most = lax.all_to_all(most, NEAR, 0, 0, tiled=True)
    most = kernel(spread_kernel, f32(lax.axis_size("gx_0"), 1, 128), (most,), mib=2)
    bounds = lax.all_to_all(most, "gx_0", 0, 0, tiled=True)

    edge = f32(5, EDGE, H, NZ)
    first_lines, last_lines = kernel(
        edge_kernel,
        (edge, edge),
        (own, x_low, x_high),
        anywhere=1,
        scratch=[pltpu.VMEM((5, BX, BY, NZ), jnp.float32), pltpu.SemaphoreType.DMA(())],
        mib=4,
    )
    y_low, y_high = both_ways(last_lines, first_lines, GY)
    wide = f32(EX, 2, EY + 2 * PAD, 128)
    scratch = pltpu.VMEM(wide.shape, jnp.float32)
    basis_out = f32(ITERS + 1, BX, 2, BY, 128)
    *operator, top, plain = kernel(
        prepare_kernel,
        (wide,) * 6 + (f32(8, 128), basis_out),
        (own, x_low, x_high, y_low, y_high),
        anywhere=1,
        scratch=[scratch] * 3 + [pltpu.VMEM((5, BX, BY, NZ), jnp.float32), pltpu.SemaphoreType.DMA(())],
        flops=30_000_000,
        mib=6,
    )

    m_low, m_high = both_ways(mirror, mirror, GX)
    edge = f32(EDGE, H, NZ)
    first_lines, last_lines = kernel(mirror_edge_kernel, (edge, edge), (mirror, m_low, m_high), mib=2)
    n_low, n_high = both_ways(last_lines, first_lines, GY)
    mirrored = kernel(
        mirror_kernel,
        basis_out,
        (mirror, m_low, m_high, n_low, n_high, *operator),
        scratch=[scratch] * 2,
        flops=20_000_000,
        mib=4,
    )
    return kernel(
        combine_kernel,
        (f32(BX, BY, NZ), f32(BX, BY, NZ)),
        (low_frac, high_frac, bounds, top, plain, mirrored),
        smem=2,
        mib=2,
        flops=3_000_000,
    )


def solution(mesh):
    torus = Mesh(mesh.devices.reshape(32, 2, 4, 2, 2), GX + GY)
    block = P(GX, GY, None)
    return jax.shard_map(
        shards,
        mesh=torus,
        in_specs=(block,) * 5 + (P(), P()),
        out_specs=(block, block),
        check_vma=False,
    )
```

```python
import jax
import jax.numpy as jnp
from jax import lax
from jax.experimental import pallas as pl
from jax.experimental.pallas import tpu as pltpu
from jax.sharding import Mesh
from jax.sharding import PartitionSpec as P


ITERS = 8
GX = ("gx_0", "gx_1")
GY = ("gy_0", "gy_1", "gy_2")
BX, BY, NZ = 8, 16, 256
H = 8
PAD = 8
EX, EY = BX + 2 * H, BY + 2 * H
NEAR = ("gx_1",) + GY
VMEM = pl.BlockSpec(memory_space=pltpu.VMEM)
SMEM = pl.BlockSpec(memory_space=pltpu.SMEM)
ANY = pl.BlockSpec(memory_space=pl.ANY)
SHARED = ((7, 1, 1), (6, 2, 2), (5, 3, 3), (16, 22, 1), (17, 21, 2), (18, 20, 3), (4, 19, 4))
EDGE = BX + len(SHARED)


def shift_pairs(n):
    up = [(i, i + 1) for i in range(n - 1)]
    return up, [(b, a) for a, b in up]


def both_ways(array_up, array_down, axes):
    up, down = shift_pairs(lax.axis_size(axes))
    return lax.ppermute(array_up, axes, up), lax.ppermute(array_down, axes, down)


def turn(x, by):
    return pltpu.roll(x, by % 128, 1)


def basis(first, second, d, cx, cy, ly, cz, lz, out):
    lane = lax.broadcasted_iota(jnp.int32, (8, 128), 1)
    at_start, at_end = lane == 0, lane == 127
    bufs = (first, second)
    for k in range(1, ITERS + 1):
        now, nxt = bufs[(k - 1) % 2], bufs[k % 2]
        for tile in range(EY // 8):
            inner = H <= 8 * tile < H + BY
            start = k if inner else k + 1
            y = PAD + 8 * tile
            if start >= EX - start or (k == ITERS and not inner):
                continue
            below = [now[start - 1, h, y : y + 8, :] for h in range(2)]
            here = [now[start, h, y : y + 8, :] for h in range(2)]
            face = [cx[start - 1, h, y : y + 8, :] for h in range(2)]
            for r in range(start, EX - start):
                above = [now[r + 1, h, y : y + 8, :] for h in range(2)]
                face_up = [cx[r, h, y : y + 8, :] for h in range(2)]
                ahead = [turn(v, -1) for v in here]
                behind = [turn(v, 1) for v in here]
                ahead[0] = jnp.where(at_end, ahead[1], ahead[0])
                behind[1] = jnp.where(at_start, behind[0], behind[1])
                for h in range(2):
                    a = d[r, h, y : y + 8, :] * here[h] - (face_up[h] * above[h] + face[h] * below[h])
                    side = cy[r, h, y : y + 8, :] * now[r, h, y + 1 : y + 9, :]
                    side = side + ly[r, h, y : y + 8, :] * now[r, h, y - 1 : y + 7, :]
                    wall = cz[r, h, y : y + 8, :] * ahead[h] + lz[r, h, y : y + 8, :] * behind[h]
                    a = a - (side + wall)
                    a = 0.5 * a if k == 1 else a - nxt[r, h, y : y + 8, :]
                    nxt[r, h, y : y + 8, :] = a
                    if inner and H <= r < H + BX:
                        out[k, r - H, h, y - PAD - H : y - PAD - H + 8, :] = a
                below, here, face = here, above, face_up
    return out


def place(ref, r, y, value):
    for h in range(2):
        ref[r, h, PAD + y : PAD + y + value.shape[0], :] = value[:, 128 * h : 128 * h + 128]


def place_sides(ref, low, high):
    for i in range(BX):
        place(ref, H + i, 0, low[i])
        place(ref, H + i, H + BY, high[i])
    for t, (a, b, n) in enumerate(SHARED, BX):
        for r, by in ((a, 0), (b, n)):
            at_low, at_high = low[t], high[t]
            if by:
                at_low, at_high = pltpu.roll(at_low, 8 - by, 0), pltpu.roll(at_high, by, 0)
            for row in {1: (0, 1), 22: (22, 23)}.get(r, (r,)):
                place(ref, row, 0, at_low)
                place(ref, row, H + BY, at_high)


def prepare_kernel(
    own, x_low, x_high, y_low, y_high, d, cx, cy, ly, cz, lz, top, out, shift, first, second, held, sem
):
    lane = lax.broadcasted_iota(jnp.int32, (8, 128), 1)
    line = lax.broadcasted_iota(jnp.int32, (8, 128), 0)
    keep = [jnp.where(lax.axis_index(axes) < lax.axis_size(axes) - 1, 1.0, 0.0) for axes in (GX, GY)]
    copy = pltpu.make_async_copy(own, held, sem)
    copy.start()
    fields = (shift, cx, cy, cz, first)
    for n, ref in enumerate(fields):
        for i in range(BX):
            place(ref, i, H, x_low[n, i])
            place(ref, H + BX + i, H, x_high[n, i])
        place_sides(ref, y_low.at[n], y_high.at[n])
    copy.wait()
    for n, ref in enumerate(fields):
        for i in range(BX):
            place(ref, H + i, H, held[n, i])
    for i in range(BX):
        for h in range(2):
            out[0, i, h] = held[4, i, :, 128 * h : 128 * h + 128]

    tiles = [PAD + 8 * t for t in range(EY // 8)]

    def diagonal(r, most):
        away = jnp.maximum(jnp.maximum(H - r, r - (H + BX - 1)), 0)
        for y in tiles:
            z = [cz[r, h, y : y + 8, :] for h in range(2)]
            behind = [turn(v, 1) for v in z]
            behind[1] = jnp.where(lane == 0, behind[0], behind[1])
            behind[0] = jnp.where(lane == 0, 0.0, behind[0])
            for h in range(2):
                lower = cy[r, h, y - 1 : y + 7, :]
                total = cx[r, h, y : y + 8, :] + cx[r - 1, h, y : y + 8, :]
                total = total + cy[r, h, y : y + 8, :] + lower + z[h] + behind[h]
                diag = shift[r, h, y : y + 8, :] + total
                d[r, h, y : y + 8, :] = diag
                ly[r, h, y : y + 8, :] = lower
                lz[r, h, y : y + 8, :] = behind[h]
                row_bound = diag + total
                if y == tiles[0]:
                    row_bound = jnp.where(line > away, row_bound, 0.0)
                if y == tiles[-1]:
                    row_bound = jnp.where(line < 7 - away, row_bound, 0.0)
                most = jnp.maximum(most, row_bound)
        return most

    most = lax.fori_loop(1, EX - 1, diagonal, jnp.zeros((8, 128), jnp.float32))
    bound = jnp.max(jnp.max(most, axis=0, keepdims=True), axis=1, keepdims=True)
    top[...] = jnp.broadcast_to(bound, top.shape)
    scale = jnp.broadcast_to(4.0 / bound, (8, 128))
    inside = scale * keep[1]

    def rescale(r, carry):
        scale_x = jnp.where(r == H + BX - 1, scale * keep[0], scale)
        for y in tiles:
            last = y - PAD + 8 == H + BY
            after = y - PAD == H + BY
            for h in range(2):
                at = (r, h, slice(y, y + 8), slice(None))
                d[at] = d[at] * scale - 2.0
                cx[at] = cx[at] * scale_x
                cy[at] = cy[at] * (jnp.where(line == 7, inside, scale) if last else scale)
                ly[at] = ly[at] * (jnp.where(line == 0, inside, scale) if after else scale)
                cz[at] = cz[at] * (scale if h == 0 else jnp.where(lane == 127, 0.0, scale))
                lz[at] = lz[at] * scale
        return carry

    lax.fori_loop(0, EX, rescale, 0)
    basis(first, second, d, cx, cy, ly, cz, lz, out)


def mirror_kernel(own, x_low, x_high, y_low, y_high, d, cx, cy, ly, cz, lz, out, first, second):
    for b, block in enumerate((x_low, own, x_high)):
        for i in range(BX):
            place(first, b * BX + i, H, block[BX - 1 - i])
    place_sides(first, y_low, y_high)
    for i in range(BX):
        for h in range(2):
            out[0, i, h] = own[BX - 1 - i, :, 128 * h : 128 * h + 128]
    basis(first, second, d, cx, cy, ly, cz, lz, out)


def pack_kernel(shift, cx, cy, cz, right_side, own, plane_x, plane_y, base, sems):
    copies = [pltpu.make_async_copy(a, own.at[n], sems.at[n]) for n, a in enumerate((shift, cx, cy, cz, right_side))]
    for copy in copies:
        copy.start()
    lane = lax.broadcasted_iota(jnp.int32, (BY, NZ), 1)
    line = lax.broadcasted_iota(jnp.int32, (BY, NZ), 0)
    copies[1].wait()
    plane_x[...] = own[1, BX - 1]
    copies[2].wait()
    for i in range(BX):
        plane_y[i : i + 1, :] = own[2, i, BY - 1 : BY, :]
    copies[0].wait()
    copies[3].wait()
    whole = jnp.zeros((BY, NZ), jnp.float32)
    for r in range(BX):
        x, y, z = own[1, r], own[2, r], own[3, r]
        if r:
            x = x + own[1, r - 1]
        y = y + jnp.where(line == 0, 0.0, pltpu.roll(y, 1, 0))
        z = z + jnp.where(lane == 0, 0.0, pltpu.roll(z, 1, 1))
        row = own[0, r] + 2.0 * (x + y + z)
        base[2 * BY + r : 2 * BY + r + 1, :] = row[0:1, :]
        if r:
            whole = jnp.maximum(whole, jnp.where(line == 0, 0.0, row))
        else:
            base[BY : 2 * BY, :] = row
    base[0:BY, :] = whole
    copies[4].wait()


def edges(row, first_lines, last_lines):
    line = lax.broadcasted_iota(jnp.int32, (H, NZ), 0)
    for i in range(BX):
        first_lines[i] = row(H + i, 0)
        last_lines[i] = row(H + i, BY - H)
    for t, (a, b, n) in enumerate(SHARED, BX):
        last_lines[t] = jnp.where(line >= n, row(a, BY - H), pltpu.roll(row(b, BY - H), n, 0))
        first_lines[t] = jnp.where(line < H - n, row(a, 0), pltpu.roll(row(b, 0), H - n, 0))


def edge_kernel(own, x_low, x_high, first_lines, last_lines, held, sem):
    copy = pltpu.make_async_copy(own, held, sem)
    copy.start()
    copy.wait()
    for n in range(5):

        def row(r, y, n=n):
            return (x_low, held, x_high)[r // BX][n, r % BX, y : y + H, :]

        edges(row, first_lines.at[n], last_lines.at[n])


def mirror_edge_kernel(own, x_low, x_high, first_lines, last_lines):
    edges(lambda r, y: (x_low, own, x_high)[r // BX][BX - 1 - r % BX, y : y + H, :], first_lines, last_lines)


def bound_kernel(base, before_x, before_y, out):
    line = lax.broadcasted_iota(jnp.int32, (BY, NZ), 0)
    row = lax.broadcasted_iota(jnp.int32, (BX, NZ), 0)
    corner = jnp.where(line == 0, before_y[0:1, :], 0.0)
    largest = jnp.maximum(base[0:BY, :], base[BY : 2 * BY, :] + 2.0 * (before_x[...] + corner))
    first = jnp.where(row == 0, 0.0, base[2 * BY :, :] + 2.0 * before_y[...])
    largest = jnp.maximum(jnp.max(largest, axis=0, keepdims=True), jnp.max(first, axis=0, keepdims=True))
    largest = jnp.max(largest, axis=1, keepdims=True)
    out[...] = jnp.broadcast_to(largest[None], out.shape)


def spread_kernel(values, out):
    most = values[0]
    for i in range(1, values.shape[0]):
        most = jnp.maximum(most, values[i])
    out[...] = jnp.broadcast_to(most[None], out.shape)


def polynomials(low, high, bound, top):
    lmin = low * bound
    lmax = high * bound
    theta = (lmax + lmin) / 2.0
    delta = (lmax - lmin) / 2.0
    sigma = theta / delta
    rho = 1.0 / sigma
    half = 0.5 * top
    zero = jnp.zeros_like(bound)
    n = ITERS + 1
    x = [zero] * n
    r = [zero + 1.0] + [zero] * ITERS
    d = [r[0] / theta] + [zero] * ITERS
    for _ in range(ITERS):
        x = [a + b for a, b in zip(x, d)]
        at = d + [zero]
        moved = [0.5 * at[1], at[0] + 0.5 * at[2]] + [0.5 * (at[k - 1] + at[k + 1]) for k in range(2, n)]
        r = [a - half * (b + c) for a, b, c in zip(r, d, moved)]
        rho_new = 1.0 / (2.0 * sigma - rho)
        by, of = rho_new * rho, 2.0 * rho_new / delta
        d = [by * a + of * b for a, b in zip(d, r)]
        rho = rho_new
    return x, r


def combine_kernel(low, high, bounds, top, plain, mirrored, pressure, residual):
    bound = bounds[0]
    for i in range(1, bounds.shape[0]):
        bound = jnp.maximum(bound, bounds[i])
    bound = jnp.broadcast_to(bound, (8, 128))
    found = [polynomials(low[f], high[f], bound, top[...]) for f in range(2)]
    sums, gaps = [], []
    for part in range(2):
        sums.append([0.5 * (a + b) for a, b in zip(found[0][part], found[1][part])])
        gaps.append([0.5 * (a - b) for a, b in zip(found[0][part], found[1][part])])

    def row(r, carry):
        for i in range(0, BY, 8):
            for h in range(2):
                p = q = None
                for k in range(ITERS + 1):
                    a = plain[k, r, h, i : i + 8, :]
                    b = mirrored[k, r, h, i : i + 8, :]
                    if k < ITERS:
                        t = sums[0][k] * a + gaps[0][k] * b
                        p = t if p is None else p + t
                    t = sums[1][k] * a + gaps[1][k] * b
                    q = t if q is None else q + t
                pressure[r, i : i + 8, 128 * h : 128 * h + 128] = p
                residual[r, i : i + 8, 128 * h : 128 * h + 128] = q
        return carry

    lax.fori_loop(0, BX, row, 0)


def f32(*shape):
    return jax.ShapeDtypeStruct(shape, jnp.float32)


def kernel(body, out, operands, smem=0, anywhere=0, scratch=(), mib=16, flops=1_000_000):
    nbytes = sum(a.size * 4 for a in operands)
    return pl.pallas_call(
        body,
        out_shape=out,
        in_specs=[SMEM] * smem + [ANY] * anywhere + [VMEM] * (len(operands) - smem - anywhere),
        out_specs=jax.tree.map(lambda _: VMEM, out),
        scratch_shapes=scratch,
        compiler_params=pltpu.CompilerParams(vmem_limit_bytes=mib << 20),
        cost_estimate=pl.CostEstimate(flops=flops, bytes_accessed=nbytes, transcendentals=0),
    )(*operands)


def shards(right_side, shift, coef_x, coef_y, coef_z, low_frac, high_frac):
    nx, ny = lax.axis_size(GX), lax.axis_size(GY)
    up_x, up_y = shift_pairs(nx)[0], shift_pairs(ny)[0]
    given = (shift, coef_x, coef_y, coef_z, right_side)

    mirror = lax.ppermute(right_side, GX, [(i, nx - 1 - i) for i in range(nx)])
    own, plane_x, plane_y, base = kernel(
        pack_kernel,
        (f32(5, BX, BY, NZ), f32(BY, NZ), f32(BX, NZ), f32(2 * BY + BX, NZ)),
        given,
        scratch=[pltpu.SemaphoreType.DMA((5,))],
        anywhere=5,
        mib=56,
    )
    before_x = lax.ppermute(plane_x, GX, up_x)
    before_y = lax.ppermute(plane_y, GY, up_y)
    x_low, x_high = both_ways(own, own, GX)

    chips_z, near = lax.axis_size("gx_0"), lax.axis_size(NEAR)
    most = kernel(bound_kernel, f32(chips_z, 1, 128), (base, before_x, before_y), mib=2)
    most = lax.all_to_all(most, "gx_0", 0, 0, tiled=True)
    most = kernel(spread_kernel, f32(near, 1, 128), (most,), mib=2)
    bounds = lax.all_to_all(most, NEAR, 0, 0, tiled=True)

    edge = f32(5, EDGE, H, NZ)
    first_lines, last_lines = kernel(
        edge_kernel,
        (edge, edge),
        (own, x_low, x_high),
        anywhere=1,
        scratch=[pltpu.VMEM((5, BX, BY, NZ), jnp.float32), pltpu.SemaphoreType.DMA(())],
        mib=4,
    )
    y_low, y_high = both_ways(last_lines, first_lines, GY)
    wide = f32(EX, 2, EY + 2 * PAD, 128)
    scratch = pltpu.VMEM(wide.shape, jnp.float32)
    basis_out = f32(ITERS + 1, BX, 2, BY, 128)
    *operator, top, plain = kernel(
        prepare_kernel,
        (wide,) * 6 + (f32(8, 128), basis_out),
        (own, x_low, x_high, y_low, y_high),
        anywhere=1,
        scratch=[scratch] * 3 + [pltpu.VMEM((5, BX, BY, NZ), jnp.float32), pltpu.SemaphoreType.DMA(())],
        flops=30_000_000,
        mib=6,
    )

    m_low, m_high = both_ways(mirror, mirror, GX)
    edge = f32(EDGE, H, NZ)
    first_lines, last_lines = kernel(mirror_edge_kernel, (edge, edge), (mirror, m_low, m_high), mib=2)
    n_low, n_high = both_ways(last_lines, first_lines, GY)
    mirrored = kernel(
        mirror_kernel,
        basis_out,
        (mirror, m_low, m_high, n_low, n_high, *operator),
        scratch=[scratch] * 2,
        flops=20_000_000,
        mib=4,
    )
    return kernel(
        combine_kernel,
        (f32(BX, BY, NZ), f32(BX, BY, NZ)),
        (low_frac, high_frac, bounds, top, plain, mirrored),
        smem=2,
        mib=2,
        flops=3_000_000,
    )


def solution(mesh):
    torus = Mesh(mesh.devices.reshape(32, 2, 4, 2, 2), GX + GY)
    block = P(GX, GY, None)
    return jax.shard_map(
        shards,
        mesh=torus,
        in_specs=(block,) * 5 + (P(), P()),
        out_specs=(block, block),
        check_vma=False,
    )
```

```python
import jax
import jax.numpy as jnp
from jax import lax
from jax.experimental import pallas as pl
from jax.experimental.pallas import tpu as pltpu
from jax.sharding import Mesh
from jax.sharding import PartitionSpec as P


ITERS = 8
GX = ("gx_0", "gx_1")
GY = ("gy_0", "gy_1", "gy_2")
BX, BY, NZ = 8, 16, 256
H = 8
PAD = 8
EX, EY = BX + 2 * H, BY + 2 * H
NEAR = ("gx_1",) + GY
VMEM = pl.BlockSpec(memory_space=pltpu.VMEM)
SMEM = pl.BlockSpec(memory_space=pltpu.SMEM)
ANY = pl.BlockSpec(memory_space=pl.ANY)
SHARED = ((7, 1, 1), (6, 2, 2), (5, 3, 3), (16, 22, 1), (17, 21, 2), (18, 20, 3), (4, 19, 4))
EDGE = BX + len(SHARED)


def shift_pairs(n):
    up = [(i, i + 1) for i in range(n - 1)]
    return up, [(b, a) for a, b in up]


def both_ways(array_up, array_down, axes):
    up, down = shift_pairs(lax.axis_size(axes))
    return lax.ppermute(array_up, axes, up), lax.ppermute(array_down, axes, down)


def turn(x, by):
    return pltpu.roll(x, by % 128, 1)


def basis(first, second, d, cx, cy, ly, cz, lz, out):
    lane = lax.broadcasted_iota(jnp.int32, (8, 128), 1)
    at_start, at_end = lane == 0, lane == 127
    bufs = (first, second)
    for k in range(1, ITERS + 1):
        now, nxt = bufs[(k - 1) % 2], bufs[k % 2]
        for tile in range(EY // 8):
            inner = H <= 8 * tile < H + BY
            start = k if inner else k + 1
            y = PAD + 8 * tile
            if start >= EX - start or (k == ITERS and not inner):
                continue
            below = [now[start - 1, h, y : y + 8, :] for h in range(2)]
            here = [now[start, h, y : y + 8, :] for h in range(2)]
            face = [cx[start - 1, h, y : y + 8, :] for h in range(2)]
            for r in range(start, EX - start):
                above = [now[r + 1, h, y : y + 8, :] for h in range(2)]
                face_up = [cx[r, h, y : y + 8, :] for h in range(2)]
                ahead = [turn(v, -1) for v in here]
                behind = [turn(v, 1) for v in here]
                ahead[0] = jnp.where(at_end, ahead[1], ahead[0])
                behind[1] = jnp.where(at_start, behind[0], behind[1])
                for h in range(2):
                    a = d[r, h, y : y + 8, :] * here[h] - (face_up[h] * above[h] + face[h] * below[h])
                    side = cy[r, h, y : y + 8, :] * now[r, h, y + 1 : y + 9, :]
                    side = side + ly[r, h, y : y + 8, :] * now[r, h, y - 1 : y + 7, :]
                    wall = cz[r, h, y : y + 8, :] * ahead[h] + lz[r, h, y : y + 8, :] * behind[h]
                    a = a - (side + wall)
                    a = 0.5 * a if k == 1 else a - nxt[r, h, y : y + 8, :]
                    nxt[r, h, y : y + 8, :] = a
                    if inner and H <= r < H + BX:
                        out[k, r - H, h, y - PAD - H : y - PAD - H + 8, :] = a
                below, here, face = here, above, face_up
    return out


def place(ref, r, y, value):
    for h in range(2):
        ref[r, h, PAD + y : PAD + y + value.shape[0], :] = value[:, 128 * h : 128 * h + 128]


def place_sides(ref, low, high):
    for i in range(BX):
        place(ref, H + i, 0, low[i])
        place(ref, H + i, H + BY, high[i])
    for t, (a, b, n) in enumerate(SHARED, BX):
        for r, by in ((a, 0), (b, n)):
            at_low, at_high = low[t], high[t]
            if by:
                at_low, at_high = pltpu.roll(at_low, 8 - by, 0), pltpu.roll(at_high, by, 0)
            for row in {1: (0, 1), 22: (22, 23)}.get(r, (r,)):
                place(ref, row, 0, at_low)
                place(ref, row, H + BY, at_high)


def prepare_kernel(
    own, x_low, x_high, y_low, y_high, d, cx, cy, ly, cz, lz, top, out, shift, first, second, held, sem
):
    lane = lax.broadcasted_iota(jnp.int32, (8, 128), 1)
    line = lax.broadcasted_iota(jnp.int32, (8, 128), 0)
    keep = [jnp.where(lax.axis_index(axes) < lax.axis_size(axes) - 1, 1.0, 0.0) for axes in (GX, GY)]
    copy = pltpu.make_async_copy(own, held, sem)
    copy.start()
    fields = (shift, cx, cy, cz, first)
    for n, ref in enumerate(fields):
        for i in range(BX):
            place(ref, i, H, x_low[n, i])
            place(ref, H + BX + i, H, x_high[n, i])
        place_sides(ref, y_low.at[n], y_high.at[n])
    copy.wait()
    for n, ref in enumerate(fields):
        for i in range(BX):
            place(ref, H + i, H, held[n, i])
    for i in range(BX):
        for h in range(2):
            out[0, i, h] = held[4, i, :, 128 * h : 128 * h + 128]

    tiles = [PAD + 8 * t for t in range(EY // 8)]

    def diagonal(r, most):
        away = jnp.maximum(jnp.maximum(H - r, r - (H + BX - 1)), 0)
        for y in tiles:
            z = [cz[r, h, y : y + 8, :] for h in range(2)]
            behind = [turn(v, 1) for v in z]
            behind[1] = jnp.where(lane == 0, behind[0], behind[1])
            behind[0] = jnp.where(lane == 0, 0.0, behind[0])
            for h in range(2):
                lower = cy[r, h, y - 1 : y + 7, :]
                total = cx[r, h, y : y + 8, :] + cx[r - 1, h, y : y + 8, :]
                total = total + cy[r, h, y : y + 8, :] + lower + z[h] + behind[h]
                diag = shift[r, h, y : y + 8, :] + total
                d[r, h, y : y + 8, :] = diag
                ly[r, h, y : y + 8, :] = lower
                lz[r, h, y : y + 8, :] = behind[h]
                row_bound = diag + total
                if y == tiles[0]:
                    row_bound = jnp.where(line > away, row_bound, 0.0)
                if y == tiles[-1]:
                    row_bound = jnp.where(line < 7 - away, row_bound, 0.0)
                most = jnp.maximum(most, row_bound)
        return most

    most = lax.fori_loop(1, EX - 1, diagonal, jnp.zeros((8, 128), jnp.float32))
    bound = jnp.max(jnp.max(most, axis=0, keepdims=True), axis=1, keepdims=True)
    top[...] = jnp.broadcast_to(bound, top.shape)
    scale = jnp.broadcast_to(4.0 / bound, (8, 128))
    inside = scale * keep[1]

    def rescale(r, carry):
        scale_x = jnp.where(r == H + BX - 1, scale * keep[0], scale)
        for y in tiles:
            last = y - PAD + 8 == H + BY
            after = y - PAD == H + BY
            for h in range(2):
                at = (r, h, slice(y, y + 8), slice(None))
                d[at] = d[at] * scale - 2.0
                cx[at] = cx[at] * scale_x
                cy[at] = cy[at] * (jnp.where(line == 7, inside, scale) if last else scale)
                ly[at] = ly[at] * (jnp.where(line == 0, inside, scale) if after else scale)
                cz[at] = cz[at] * (scale if h == 0 else jnp.where(lane == 127, 0.0, scale))
                lz[at] = lz[at] * scale
        return carry

    lax.fori_loop(0, EX, rescale, 0)
    basis(first, second, d, cx, cy, ly, cz, lz, out)


def mirror_kernel(own, x_low, x_high, y_low, y_high, d, cx, cy, ly, cz, lz, out, first, second):
    for b, block in enumerate((x_low, own, x_high)):
        for i in range(BX):
            place(first, b * BX + i, H, block[BX - 1 - i])
    place_sides(first, y_low, y_high)
    for i in range(BX):
        for h in range(2):
            out[0, i, h] = own[BX - 1 - i, :, 128 * h : 128 * h + 128]
    basis(first, second, d, cx, cy, ly, cz, lz, out)


def pack_kernel(shift, cx, cy, cz, right_side, own, plane_x, plane_y, base, sems):
    copies = [pltpu.make_async_copy(a, own.at[n], sems.at[n]) for n, a in enumerate((shift, cx, cy, cz, right_side))]
    for copy in copies:
        copy.start()
    lane = lax.broadcasted_iota(jnp.int32, (BY, NZ), 1)
    line = lax.broadcasted_iota(jnp.int32, (BY, NZ), 0)
    copies[1].wait()
    plane_x[...] = own[1, BX - 1]
    copies[2].wait()
    for i in range(BX):
        plane_y[i : i + 1, :] = own[2, i, BY - 1 : BY, :]
    copies[0].wait()
    copies[3].wait()
    whole = jnp.zeros((BY, NZ), jnp.float32)
    for r in range(BX):
        x, y, z = own[1, r], own[2, r], own[3, r]
        if r:
            x = x + own[1, r - 1]
        y = y + jnp.where(line == 0, 0.0, pltpu.roll(y, 1, 0))
        z = z + jnp.where(lane == 0, 0.0, pltpu.roll(z, 1, 1))
        row = own[0, r] + 2.0 * (x + y + z)
        base[2 * BY + r : 2 * BY + r + 1, :] = row[0:1, :]
        if r:
            whole = jnp.maximum(whole, jnp.where(line == 0, 0.0, row))
        else:
            base[BY : 2 * BY, :] = row
    base[0:BY, :] = whole
    copies[4].wait()


def edges(row, first_lines, last_lines):
    line = lax.broadcasted_iota(jnp.int32, (H, NZ), 0)
    for i in range(BX):
        first_lines[i] = row(H + i, 0)
        last_lines[i] = row(H + i, BY - H)
    for t, (a, b, n) in enumerate(SHARED, BX):
        last_lines[t] = jnp.where(line >= n, row(a, BY - H), pltpu.roll(row(b, BY - H), n, 0))
        first_lines[t] = jnp.where(line < H - n, row(a, 0), pltpu.roll(row(b, 0), H - n, 0))


def edge_kernel(own, x_low, x_high, first_lines, last_lines, held, sem):
    copy = pltpu.make_async_copy(own, held, sem)
    copy.start()
    copy.wait()
    for n in range(5):

        def row(r, y, n=n):
            return (x_low, held, x_high)[r // BX][n, r % BX, y : y + H, :]

        edges(row, first_lines.at[n], last_lines.at[n])


def mirror_edge_kernel(own, x_low, x_high, first_lines, last_lines):
    edges(lambda r, y: (x_low, own, x_high)[r // BX][BX - 1 - r % BX, y : y + H, :], first_lines, last_lines)


def bound_kernel(base, before_x, before_y, out):
    line = lax.broadcasted_iota(jnp.int32, (BY, NZ), 0)
    row = lax.broadcasted_iota(jnp.int32, (BX, NZ), 0)
    corner = jnp.where(line == 0, before_y[0:1, :], 0.0)
    largest = jnp.maximum(base[0:BY, :], base[BY : 2 * BY, :] + 2.0 * (before_x[...] + corner))
    first = jnp.where(row == 0, 0.0, base[2 * BY :, :] + 2.0 * before_y[...])
    largest = jnp.maximum(jnp.max(largest, axis=0, keepdims=True), jnp.max(first, axis=0, keepdims=True))
    largest = jnp.max(largest, axis=1, keepdims=True)
    out[...] = jnp.broadcast_to(largest[None], out.shape)


def spread_kernel(values, out):
    most = values[0]
    for i in range(1, values.shape[0]):
        most = jnp.maximum(most, values[i])
    out[...] = jnp.broadcast_to(most[None], out.shape)


def polynomials(low, high, bound, top):
    lmin = low * bound
    lmax = high * bound
    theta = (lmax + lmin) / 2.0
    delta = (lmax - lmin) / 2.0
    sigma = theta / delta
    rho = 1.0 / sigma
    half = 0.5 * top
    zero = jnp.zeros_like(bound)
    n = ITERS + 1
    x = [zero] * n
    r = [zero + 1.0] + [zero] * ITERS
    d = [r[0] / theta] + [zero] * ITERS
    for _ in range(ITERS):
        x = [a + b for a, b in zip(x, d)]
        at = d + [zero]
        moved = [0.5 * at[1], at[0] + 0.5 * at[2]] + [0.5 * (at[k - 1] + at[k + 1]) for k in range(2, n)]
        r = [a - half * (b + c) for a, b, c in zip(r, d, moved)]
        rho_new = 1.0 / (2.0 * sigma - rho)
        by, of = rho_new * rho, 2.0 * rho_new / delta
        d = [by * a + of * b for a, b in zip(d, r)]
        rho = rho_new
    return x, r


def combine_kernel(low, high, bounds, top, plain, mirrored, pressure, residual):
    bound = bounds[0]
    for i in range(1, bounds.shape[0]):
        bound = jnp.maximum(bound, bounds[i])
    bound = jnp.broadcast_to(bound, (8, 128))
    found = [polynomials(low[f], high[f], bound, top[...]) for f in range(2)]
    sums, gaps = [], []
    for part in range(2):
        sums.append([0.5 * (a + b) for a, b in zip(found[0][part], found[1][part])])
        gaps.append([0.5 * (a - b) for a, b in zip(found[0][part], found[1][part])])

    def row(r, carry):
        for i in range(0, BY, 8):
            for h in range(2):
                p = q = None
                for k in range(ITERS + 1):
                    a = plain[k, r, h, i : i + 8, :]
                    b = mirrored[k, r, h, i : i + 8, :]
                    if k < ITERS:
                        t = sums[0][k] * a + gaps[0][k] * b
                        p = t if p is None else p + t
                    t = sums[1][k] * a + gaps[1][k] * b
                    q = t if q is None else q + t
                pressure[r, i : i + 8, 128 * h : 128 * h + 128] = p
                residual[r, i : i + 8, 128 * h : 128 * h + 128] = q
        return carry

    lax.fori_loop(0, BX, row, 0)


def f32(*shape):
    return jax.ShapeDtypeStruct(shape, jnp.float32)


def kernel(body, out, operands, smem=0, anywhere=0, scratch=(), mib=16, flops=1_000_000):
    nbytes = sum(a.size * 4 for a in operands)
    return pl.pallas_call(
        body,
        out_shape=out,
        in_specs=[SMEM] * smem + [ANY] * anywhere + [VMEM] * (len(operands) - smem - anywhere),
        out_specs=jax.tree.map(lambda _: VMEM, out),
        scratch_shapes=scratch,
        compiler_params=pltpu.CompilerParams(vmem_limit_bytes=mib << 20),
        cost_estimate=pl.CostEstimate(flops=flops, bytes_accessed=nbytes, transcendentals=0),
    )(*operands)


def shards(right_side, shift, coef_x, coef_y, coef_z, low_frac, high_frac):
    nx, ny = lax.axis_size(GX), lax.axis_size(GY)
    up_x, up_y = shift_pairs(nx)[0], shift_pairs(ny)[0]
    given = (shift, coef_x, coef_y, coef_z, right_side)

    mirror = lax.ppermute(right_side, GX, [(i, nx - 1 - i) for i in range(nx)])
    own, plane_x, plane_y, base = kernel(
        pack_kernel,
        (f32(5, BX, BY, NZ), f32(BY, NZ), f32(BX, NZ), f32(2 * BY + BX, NZ)),
        given,
        scratch=[pltpu.SemaphoreType.DMA((5,))],
        anywhere=5,
        mib=56,
    )
    before_x = lax.ppermute(plane_x, GX, up_x)
    before_y = lax.ppermute(plane_y, GY, up_y)
    x_low, x_high = both_ways(own, own, GX)

    chips_z, near = lax.axis_size("gx_0"), lax.axis_size(NEAR)
    most = kernel(bound_kernel, f32(near, 1, 128), (base, before_x, before_y), mib=2)
    most = lax.all_to_all(most, NEAR, 0, 0, tiled=True)
    most = kernel(spread_kernel, f32(chips_z, 1, 128), (most,), mib=2)
    bounds = lax.all_to_all(most, "gx_0", 0, 0, tiled=True)

    edge = f32(5, EDGE, H, NZ)
    first_lines, last_lines = kernel(
        edge_kernel,
        (edge, edge),
        (own, x_low, x_high),
        anywhere=1,
        scratch=[pltpu.VMEM((5, BX, BY, NZ), jnp.float32), pltpu.SemaphoreType.DMA(())],
        mib=4,
    )
    y_low, y_high = both_ways(last_lines, first_lines, GY)
    wide = f32(EX, 2, EY + 2 * PAD, 128)
    scratch = pltpu.VMEM(wide.shape, jnp.float32)
    basis_out = f32(ITERS + 1, BX, 2, BY, 128)
    *operator, top, plain = kernel(
        prepare_kernel,
        (wide,) * 6 + (f32(8, 128), basis_out),
        (own, x_low, x_high, y_low, y_high),
        anywhere=1,
        scratch=[scratch] * 3 + [pltpu.VMEM((5, BX, BY, NZ), jnp.float32), pltpu.SemaphoreType.DMA(())],
        flops=30_000_000,
        mib=6,
    )

    m_low, m_high = both_ways(mirror, mirror, GX)
    edge = f32(EDGE, H, NZ)
    first_lines, last_lines = kernel(mirror_edge_kernel, (edge, edge), (mirror, m_low, m_high), mib=2)
    n_low, n_high = both_ways(last_lines, first_lines, GY)
    mirrored = kernel(
        mirror_kernel,
        basis_out,
        (mirror, m_low, m_high, n_low, n_high, *operator),
        scratch=[scratch] * 2,
        flops=20_000_000,
        mib=4,
    )
    return kernel(
        combine_kernel,
        (f32(BX, BY, NZ), f32(BX, BY, NZ)),
        (low_frac, high_frac, bounds, top, plain, mirrored),
        smem=2,
        mib=2,
        flops=3_000_000,
    )


def solution(mesh):
    torus = Mesh(mesh.devices.reshape(32, 2, 4, 2, 2), GX + GY)
    block = P(GX, GY, None)
    return jax.shard_map(
        shards,
        mesh=torus,
        in_specs=(block,) * 5 + (P(), P()),
        out_specs=(block, block),
        check_vma=False,
    )
```
